32 devices in a mesh: gx: 8 (over z, core), gy: 4 (over y, x).
Axes of the slice: x: 2, y: 2, z: 4, core: 2. Of those that a mesh axis runs over, the one named last changes fastest.
Arguments:
- rhs: float32 [64, 32, 6, 3, 256], P('gx', 'gy'), may hold values from -400 to 400
- contrast: float32 [64, 32, 256], P('gx', 'gy'), may hold values from 0.2 to 2
- occupied: int32 [64, 32], P('gx', 'gy'), may hold values 0 or 1
- near: bfloat16 [5, 768, 768], replicated, may hold values from -0.078125 to 0.078125
- basis: bfloat16 [768, 64], replicated, may hold values from -0.21875 to 0.21875
- transfer: float32 [4, 4, 64, 64], replicated, may hold values from -0.5 to 0.5
- coupling: float32 [5, 20, 64, 64], replicated, may hold values from -0.15625 to 0.15625
Outputs:
- third: float32 [64, 32, 6, 3, 256], P('gx', 'gy')
- hess: float32 [6, 6], replicated
The draws below stay inside these ranges and needn't reach their ends.
All inputs are finite; a program needn't handle non-finite values. No bound on the sum of `occupied` on one device may be relied on, other than what follows from the above.
Results may differ from the reference program's by a relative error of at most 0.0031.
Values may be sent and summed in bfloat16 or wider, within the bound.
A program may use at most 128 MiB of HBM per device.

```python
import math
import jax
import jax.numpy as jnp
from jax import lax

P_SIZE = 256
R = 64
NRHS = 6
NLX = 64
NLY = 32
LEVELS = 5


def draw_rhs(key, part):
    key_base = jax.random.fold_in(key, 11)
    key_values, key_box, key_voxel = jax.random.split(key_base, 3)
    shape_all = (NLX, NLY, NRHS, 3, P_SIZE)
    values_drawn = jnp.clip(jax.random.normal(key_values, shape_all, jnp.float32), -4.0, 4.0)
    box_scale = jnp.exp(math.log(10.0) * jax.random.uniform(key_box, (NLX, NLY), jnp.float32))
    rising = 1.0 + 2.0 * jnp.arange(NLX, dtype=jnp.float32) / NLX
    voxel_scale = jnp.exp(math.log(3.0) * jax.random.uniform(key_voxel, (P_SIZE,), jnp.float32))
    return values_drawn * (box_scale * rising[:, None])[:, :, None, None, None] * voxel_scale


def touch_ends(drawn, own_key, low, largest):
    spot = [jax.random.randint(jax.random.fold_in(own_key, axis), (), 0, length) for axis, length in enumerate(drawn.shape)]
    widest = drawn.shape.index(max(drawn.shape))
    next_to = spot[:widest] + [(spot[widest] + 1) % drawn.shape[widest]] + spot[widest + 1:]
    return drawn.at[tuple(spot)].set(low).at[tuple(next_to)].set(largest)


def levels(rng, dims, pieces, least, largest):
    loudness, own = 1.0, jax.random.fold_in(rng, 6)
    for axis_at, blocks in pieces:
        steps = jnp.exp(jax.random.uniform(jax.random.fold_in(own, axis_at), (blocks,), jnp.float32, least / len(pieces), largest / len(pieces)))
        loudness = loudness * jnp.repeat(steps, dims[axis_at] // blocks).reshape([-1 if axis == axis_at else 1 for axis in range(len(dims))])
    return loudness


def gaussian(stream_key, extent, scale, bound, kind=jnp.bfloat16):
    return jnp.clip(scale * jax.random.normal(stream_key, extent, jnp.float32), -bound, bound).astype(kind)


def setup_inputs(seed: int = 0) -> dict:
    keys = jax.random.split(jax.random.key(seed), 8)
    return {
        "rhs": draw_rhs(jax.random.fold_in(keys[7], 71), 0),
        "contrast": jnp.clip(jnp.exp(math.log(2.0) - 2.3025851 * jax.random.uniform(keys[1], (NLX, NLY, P_SIZE), jnp.float32) ** levels(keys[1], (NLX, NLY, P_SIZE), ((0, 8), (1, 4)), -0.2, 0.2)), 0.2, 2.0),
        "occupied": touch_ends((jax.random.randint(keys[2], (NLX, NLY), 0, 4) < 3).astype(jnp.int32), jax.random.fold_in(keys[2], 1), 0, 1),
        "near": gaussian(keys[3], (5, 3 * P_SIZE, 3 * P_SIZE), (27 * P_SIZE) ** -0.5, 0.078125),
        "basis": gaussian(keys[4], (3 * P_SIZE, R), (3 * P_SIZE) ** -0.5, 0.21875),
        "transfer": gaussian(keys[5], (LEVELS - 1, 4, R, R), (2 * R) ** -0.5, 0.5, jnp.float32),
        "coupling": gaussian(keys[6], (LEVELS, 20, R, R), (27 * R) ** -0.5, 0.15625, jnp.float32),
    }


PRECISE = lax.Precision.HIGHEST
EPSILON = 1e-06
NEAR_BASE = ((0, 0), (1, -1), (1, 0), (1, 1), (0, 1))

def near_terms():
    listing = []
    for slot_index, (shift_x, shift_y) in enumerate(NEAR_BASE):
        listing.append((shift_x, shift_y, slot_index, False))
        if shift_x != 0 or shift_y != 0:
            listing.append((-shift_x, -shift_y, slot_index, True))
    return listing

def far_terms():
    base_list = []
    for shift_x in range(-3, 4):
        for shift_y in range(-3, 4):
            if max(abs(shift_x), abs(shift_y)) >= 2 and (shift_x > 0 or (shift_x == 0 and shift_y > 0)):
                base_list.append((shift_x, shift_y))
    listing = []
    for slot_index, (shift_x, shift_y) in enumerate(base_list):
        listing.append((shift_x, shift_y, slot_index, False))
        listing.append((-shift_x, -shift_y, slot_index, True))
    return listing

def parent_close(parity, offset):
    return jnp.abs((parity + offset) // 2) <= 1

def lift(skeleton, matrices):
    size_x, size_y, fields, rank = skeleton.shape
    fold_x = 2 if size_x > 1 else 1
    fold_y = 2 if size_y > 1 else 1
    blocks = skeleton.reshape(size_x // fold_x, fold_x, size_y // fold_y, fold_y, fields, rank)
    total = jnp.zeros((size_x // fold_x, size_y // fold_y, fields, rank), jnp.float32)
    for child_x in range(fold_x):
        for child_y in range(fold_y):
            piece = blocks[:, child_x, :, child_y].reshape(-1, rank)
            total = total + jnp.dot(piece, matrices[2 * child_x + child_y], precision=PRECISE).reshape(total.shape)
    return total

def lower(parent, matrices, size_x, size_y):
    par_x, par_y, fields, rank = parent.shape
    fold_x = size_x // par_x
    fold_y = size_y // par_y
    flat_parent = parent.reshape(-1, rank)
    rows_list = []
    for child_x in range(fold_x):
        cols_list = []
        for child_y in range(fold_y):
            cols_list.append(jnp.dot(flat_parent, matrices[2 * child_x + child_y].T, precision=PRECISE).reshape(parent.shape))
        rows_list.append(jnp.stack(cols_list, axis=2))
    return jnp.stack(rows_list, axis=1).reshape(size_x, size_y, fields, rank)

def couple_padded(padded, size_x, size_y, matrices):
    fields, rank = (padded.shape[2], padded.shape[3])
    parity_x = jnp.arange(size_x, dtype=jnp.int32) % 2
    parity_y = jnp.arange(size_y, dtype=jnp.int32) % 2
    total = jnp.zeros((size_x, size_y, fields, rank), jnp.float32)
    for shift_x, shift_y, slot_index, flipped in far_terms():
        block = matrices[slot_index].T if flipped else matrices[slot_index]
        piece = padded[3 + shift_x:3 + shift_x + size_x, 3 + shift_y:3 + shift_y + size_y].reshape(-1, rank)
        keep = (parent_close(parity_x, shift_x)[:, None] & parent_close(parity_y, shift_y)[None, :]).astype(jnp.float32)
        total = total + keep[:, :, None, None] * jnp.dot(piece, block, precision=PRECISE).reshape(size_x, size_y, fields, rank)
    return total

def couple(skeleton, matrices):
    padded = jnp.pad(skeleton, ((3, 3), (3, 3), (0, 0), (0, 0)))
    return couple_padded(padded, skeleton.shape[0], skeleton.shape[1], matrices)

def apply_operator(field, occupied, contrast, near, basis, transfer, coupling):
    source = (occupied.astype(jnp.float32)[:, :, None, None, None] * contrast[:, :, None, None, :] * field).astype(jnp.bfloat16)
    size_x, size_y, fields = (source.shape[0], source.shape[1], source.shape[2])
    width = source.shape[3] * source.shape[4]
    rank = basis.shape[1]
    flat_source = source.reshape(size_x, size_y, fields, width)
    padded = jnp.pad(flat_source, ((1, 1), (1, 1), (0, 0), (0, 0)))
    near_sum = jnp.zeros((size_x, size_y, fields, width), jnp.float32)
    for shift_x, shift_y, slot_index, flipped in near_terms():
        block = near[slot_index].T if flipped else near[slot_index]
        piece = padded[1 + shift_x:1 + shift_x + size_x, 1 + shift_y:1 + shift_y + size_y].reshape(-1, width)
        near_sum = near_sum + jnp.dot(piece, block, preferred_element_type=jnp.float32).reshape(size_x, size_y, fields, width)
    skeleton = [jnp.dot(flat_source.reshape(-1, width), basis, preferred_element_type=jnp.float32).reshape(size_x, size_y, fields, rank)]
    for depth in range(LEVELS - 1):
        skeleton.append(lift(skeleton[-1], transfer[depth]))
    down = couple(skeleton[LEVELS - 1], coupling[LEVELS - 1])
    for depth in range(LEVELS - 2, -1, -1):
        child = skeleton[depth]
        down = couple(child, coupling[depth]) + lower(down, transfer[depth], child.shape[0], child.shape[1])
    far_part = jnp.dot(down.reshape(-1, rank), basis.T.astype(jnp.float32), precision=PRECISE).reshape(size_x, size_y, fields, width)
    return field + (near_sum + far_part).reshape(field.shape)

def reference(rhs, contrast, occupied, near, basis, transfer, coupling):

    def inner(first_arr, second_arr):
        return lax.optimization_barrier(jnp.mean(first_arr * second_arr, axis=(0, 1, 3, 4)))

    def spread(values):
        return values[None, None, :, None, None]

    def operate(field):
        return apply_operator(field, occupied, contrast, near, basis, transfer, coupling)
    scale_start = jnp.sqrt(inner(rhs, rhs) + EPSILON)
    first = rhs / spread(scale_start)
    image = operate(first)
    coef_first = inner(first, image)
    rest = image - spread(coef_first) * first
    norm_first = jnp.sqrt(inner(rest, rest) + EPSILON)
    second = rest / spread(norm_first)
    image = operate(second)
    coef_cross = inner(first, image)
    coef_second = inner(second, image)
    rest = image - spread(coef_cross) * first - spread(coef_second) * second
    norm_second = jnp.sqrt(inner(rest, rest) + EPSILON)
    third = rest / spread(norm_second)
    hess = jnp.stack([scale_start, coef_first, norm_first, coef_cross, coef_second, norm_second], axis=1)
    return (third, hess)
```

```python
import functools

import jax
import jax.numpy as jnp
from jax import lax
from jax.experimental import pallas as pl
from jax.experimental.pallas import tpu as pltpu
from jax.sharding import PartitionSpec as P

PRECISE = lax.Precision.HIGH
EPSILON = 1e-06
NEAR_BASE = ((0, 0), (1, -1), (1, 0), (1, 1), (0, 1))
AROUND = [(a, b) for a in (-1, 0, 1) for b in (-1, 0, 1)]
COMPASS = [d for d in AROUND if d != (0, 0)]
MESH = pl.DeviceIdType.MESH
VMEM = pl.BlockSpec(memory_space=pltpu.VMEM)


def near_lookup():
    table = {}
    for slot, (a, b) in enumerate(NEAR_BASE):
        table[(a, b)] = (slot, False)
        if (a, b) != (0, 0):
            table[(-a, -b)] = (slot, True)
    return table


def far_lookup():
    base = [
        (a, b)
        for a in range(-3, 4)
        for b in range(-3, 4)
        if max(abs(a), abs(b)) >= 2 and (a > 0 or (a == 0 and b > 0))
    ]
    table = {}
    for slot, (a, b) in enumerate(base):
        table[(a, b)] = (slot, False)
        table[(-a, -b)] = (slot, True)
    return table


def far_kernel(coupling, out):
    table = far_lookup()
    rank = coupling.shape[2]
    children = [(c, e) for c in (0, 1) for e in (0, 1)]
    empty = jnp.zeros((rank, rank), jnp.float32)
    row = 0
    for px, py in AROUND:
        for c, e in children:
            line = []
            for tc, te in children:
                found = table.get((2 * px + c - tc, 2 * py + e - te))
                if found is None:
                    line.append(empty)
                else:
                    block = coupling[0, found[0]]
                    line.append(block.T if found[1] else block)
            out[0, row : row + rank, :] = jnp.concatenate(line, axis=1)
            row += rank


def far_matrices(coupling):
    levels, slots, rank, _ = coupling.shape
    return pl.pallas_call(
        far_kernel,
        grid=(levels,),
        in_specs=[pl.BlockSpec((1, slots, rank, rank), lambda i: (i, 0, 0, 0))],
        out_specs=pl.BlockSpec((1, 36 * rank, 4 * rank), lambda i: (i, 0, 0)),
        out_shape=jax.ShapeDtypeStruct((levels, 36 * rank, 4 * rank), jnp.float32),
    )(coupling)


def place(index, size_y):
    return {"gx": index // size_y, "gy": index % size_y}


def greet_all(size_x, size_y):
    total = size_x * size_y
    me = lax.axis_index("gx") * size_y + lax.axis_index("gy")
    barrier = pltpu.get_barrier_semaphore()

    def greet(step, carry):
        other = (me + step) % total
        pl.semaphore_signal(
            barrier, inc=1, device_id=place(other, size_y), device_id_type=MESH
        )
        return carry

    lax.fori_loop(1, total, greet, 0)
    pl.semaphore_wait(barrier, total - 1)


def gather_copy(source, target, send, receive, step, size_x, size_y):
    total = size_x * size_y
    me = lax.axis_index("gx") * size_y + lax.axis_index("gy")
    other = (me + step) % total
    return pltpu.make_async_remote_copy(
        src_ref=source,
        dst_ref=target.at[me],
        send_sem=send.at[step],
        recv_sem=receive.at[step],
        device_id=place(other, size_y),
        device_id_type=MESH,
    )


def sum_kernel(size_x, size_y, part, out, slots, send, receive):
    total = size_x * size_y
    me = lax.axis_index("gx") * size_y + lax.axis_index("gy")
    greet_all(size_x, size_y)

    def begin(step, carry):
        gather_copy(part, slots, send, receive, step, size_x, size_y).start()
        return carry

    def finish(step, carry):
        source = (me + total - step) % total
        pltpu.make_async_remote_copy(
            src_ref=part,
            dst_ref=slots.at[source],
            send_sem=send.at[step],
            recv_sem=receive.at[step],
            device_id=place((me + step) % total, size_y),
            device_id_type=MESH,
        ).wait()
        return carry

    lax.fori_loop(1, total, begin, 0)
    slots[me] = part[...]
    lax.fori_loop(1, total, finish, 0)
    out[...] = jnp.sum(slots[...], axis=0)


def sum_all(values, size_x, size_y):
    rows, columns = values.shape
    part = jnp.pad(values, ((0, 8 - rows), (0, 128 - columns)))
    total = size_x * size_y
    summed = pl.pallas_call(
        functools.partial(sum_kernel, size_x, size_y),
        in_specs=[VMEM],
        out_specs=VMEM,
        out_shape=jax.ShapeDtypeStruct((8, 128), jnp.float32),
        scratch_shapes=[
            pltpu.VMEM((total, 8, 128), jnp.float32),
            pltpu.SemaphoreType.DMA((total,)),
            pltpu.SemaphoreType.DMA((total,)),
        ],
        compiler_params=pltpu.CompilerParams(collective_id=0, has_side_effects=True),
    )(part)
    return summed[:rows, :columns]


def strip(move, length):
    if move > 0:
        return pl.ds(length - 1, 1), pl.ds(0, 1)
    if move < 0:
        return pl.ds(0, 1), pl.ds(length + 1, 1)
    return pl.ds(0, length), pl.ds(1, length)


def exchange_kernel(size_x, size_y, halos, *refs):
    inputs = refs[:halos]
    top = refs[halos]
    outputs = refs[halos + 1 : 2 * halos + 1]
    gathered = refs[2 * halos + 1]
    send, receive, gather_send, gather_receive = refs[2 * halos + 2 :]
    total = size_x * size_y
    me_x, me_y = lax.axis_index("gx"), lax.axis_index("gy")
    me = me_x * size_y + me_y
    for out in outputs:
        long_x, long_y = out.shape[0], out.shape[1]
        line_x = jnp.zeros((1,) + out.shape[1:], out.dtype)
        line_y = jnp.zeros((long_x, 1) + out.shape[2:], out.dtype)
        out[0:1] = line_x
        out[long_x - 1 : long_x] = line_x
        out[:, 0:1] = line_y
        out[:, long_y - 1 : long_y] = line_y
    greet_all(size_x, size_y)

    def copy_of(number, way):
        move_x, move_y = COMPASS[way]
        source, target = inputs[number], outputs[number]
        from_x, to_x = strip(move_x, source.shape[0])
        from_y, to_y = strip(move_y, source.shape[1])
        return pltpu.make_async_remote_copy(
            src_ref=source.at[from_x, from_y],
            dst_ref=target.at[to_x, to_y],
            send_sem=send.at[number, way],
            recv_sem=receive.at[number, way],
            device_id={"gx": me_x + move_x, "gy": me_y + move_y},
            device_id_type=MESH,
        )

    def inside(place_x, place_y):
        return (place_x >= 0) & (place_x < size_x) & (place_y >= 0) & (place_y < size_y)

    for way, (move_x, move_y) in enumerate(COMPASS):

        @pl.when(inside(me_x + move_x, me_y + move_y))
        def _(way=way):
            for number in range(halos):
                copy_of(number, way).start()

    def begin(step, carry):
        gather_copy(top, gathered, gather_send, gather_receive, step, size_x, size_y).start()
        return carry

    lax.fori_loop(1, total, begin, 0)
    gathered[me] = top[...]
    for source, target in zip(inputs, outputs):
        target[1 : 1 + source.shape[0], 1 : 1 + source.shape[1]] = source[...]

    for way, (move_x, move_y) in enumerate(COMPASS):

        @pl.when(inside(me_x + move_x, me_y + move_y))
        def _(way=way):
            for number in range(halos):
                copy_of(number, way).wait_send()

        @pl.when(inside(me_x - move_x, me_y - move_y))
        def _(way=way):
            for number in range(halos):
                copy_of(number, way).wait_recv()

    def finish(step, carry):
        source = (me + total - step) % total
        pltpu.make_async_remote_copy(
            src_ref=top,
            dst_ref=gathered.at[source],
            send_sem=gather_send.at[step],
            recv_sem=gather_receive.at[step],
            device_id=place((me + step) % total, size_y),
            device_id_type=MESH,
        ).wait()
        return carry

    lax.fori_loop(1, total, finish, 0)


def exchange(arrays, top, size_x, size_y):
    halos = len(arrays)
    total = size_x * size_y
    shapes = [
        jax.ShapeDtypeStruct((a.shape[0] + 2, a.shape[1] + 2) + a.shape[2:], a.dtype)
        for a in arrays
    ]
    shapes.append(jax.ShapeDtypeStruct((total,) + top.shape, top.dtype))
    results = pl.pallas_call(
        functools.partial(exchange_kernel, size_x, size_y, halos),
        in_specs=[VMEM] * (halos + 1),
        out_specs=[VMEM] * (halos + 1),
        out_shape=shapes,
        scratch_shapes=[
            pltpu.SemaphoreType.DMA((halos, len(COMPASS))),
            pltpu.SemaphoreType.DMA((halos, len(COMPASS))),
            pltpu.SemaphoreType.DMA((total,)),
            pltpu.SemaphoreType.DMA((total,)),
        ],
        compiler_params=pltpu.CompilerParams(collective_id=1, has_side_effects=True),
    )(*arrays, top)
    return results[:-1], results[-1]


def group(boxes):
    size_x, size_y, fields, rank = boxes.shape
    split = boxes.reshape(size_x // 2, 2, size_y // 2, 2, fields, rank)
    return split.transpose(0, 2, 4, 1, 3, 5).reshape(size_x // 2, size_y // 2, fields, 4 * rank)


def ungroup(parents):
    size_x, size_y, fields, wide = parents.shape
    split = parents.reshape(size_x, size_y, fields, 2, 2, wide // 4)
    return split.transpose(0, 3, 1, 4, 2, 5).reshape(2 * size_x, 2 * size_y, fields, wide // 4)


def times(left, right):
    rows = left.reshape(-1, left.shape[-1])
    return jnp.dot(rows, right, precision=PRECISE).reshape(left.shape[:-1] + right.shape[1:])


def windows(padded):
    size_x, size_y = padded.shape[0] - 2, padded.shape[1] - 2
    pieces = [padded[1 + a : 1 + a + size_x, 1 + b : 1 + b + size_y] for a, b in AROUND]
    return jnp.concatenate(pieces, axis=-1)


def body(rhs, contrast, occupied, near, basis, transfer, coupling):
    shape = rhs.shape
    side, _, fields, parts, voxels = shape
    width = parts * voxels
    rank = basis.shape[1]
    levels = transfer.shape[0] + 1
    inner_levels = side.bit_length() - 1
    coarse = levels - inner_levels
    devices_x = lax.axis_size("gx")
    devices_y = lax.axis_size("gy")
    place_x = lax.axis_index("gx")
    place_y = lax.axis_index("gy")
    count = float(side * side * devices_x * devices_y * width)
    rhs = rhs.reshape(side, side, fields, width)
    weight = occupied.astype(jnp.float32)[:, :, None] * contrast
    weight = jnp.tile(weight, (1, 1, parts))[:, :, None, :]
    basis_wide = basis.T.astype(jnp.float32)
    lifts = transfer.reshape(levels - 1, 4 * rank, rank)
    lowers = lifts.transpose(0, 2, 1)
    far = far_matrices(coupling)
    table = near_lookup()

    def upper_part(gathered):
        chain = [gathered.reshape(devices_x, devices_y, fields, rank)]
        for step in range(coarse - 1):
            chain.append(times(group(chain[-1]), lifts[inner_levels + step]))
        down = None
        for step in range(coarse - 1, -1, -1):
            parents = jnp.pad(group(chain[step]), ((1, 1), (1, 1), (0, 0), (0, 0)))
            own = lax.dynamic_slice(
                parents,
                (place_x >> step + 1, place_y >> step + 1, 0, 0),
                (3, 3) + parents.shape[2:],
            )
            total = times(windows(own), far[inner_levels + step])
            if down is not None:
                total = total + times(down, lowers[inner_levels + step])
            child = 2 * (place_x >> step & 1) + (place_y >> step & 1)
            down = lax.dynamic_index_in_dim(
                total.reshape(1, 1, fields, 4, rank), child, 3, keepdims=False
            )
        return down

    def operate(field):
        source = (weight * field).astype(jnp.bfloat16)
        level = jnp.dot(
            source.reshape(-1, width), basis, preferred_element_type=jnp.float32
        ).reshape(side, side, fields, rank)
        parents = []
        for depth in range(inner_levels):
            parents.append(group(level))
            level = times(parents[-1], lifts[depth])
        padded, gathered = exchange([source] + parents, level.reshape(fields, rank), devices_x, devices_y)
        down = upper_part(gathered)
        for depth in range(inner_levels - 1, -1, -1):
            local = times(windows(padded[1 + depth]), far[depth])
            down = ungroup(local + times(down, lowers[depth]))
        total = times(down, basis_wide)
        for a, b in AROUND:
            slot, flipped = table[(a, b)]
            block = near[slot].T if flipped else near[slot]
            piece = padded[0][1 + a : 1 + a + side, 1 + b : 1 + b + side].reshape(-1, width)
            total = total + jnp.dot(piece, block, preferred_element_type=jnp.float32).reshape(
                total.shape
            )
        return field + total

    def local_sum(one, other):
        return jnp.sum(one * other, axis=(0, 1, 3))

    def sums(*pairs):
        values = jnp.stack([local_sum(one, other) for one, other in pairs], axis=1)
        summed = sum_all(values, devices_x, devices_y)
        return [summed[:, i] for i in range(len(pairs))]

    def spread(values):
        return values[None, None, :, None]

    (square,) = sums((rhs, rhs))
    scale_start = jnp.sqrt(square / count + EPSILON)
    first = rhs / spread(scale_start)
    image = operate(first)
    total_proj, total_square = sums((first, image), (image, image))
    coef_first = total_proj / count
    norm_first = jnp.sqrt(total_square / count - coef_first * coef_first + EPSILON)
    second = (image - spread(coef_first) * first) / spread(norm_first)
    image = operate(second)
    total_cross, total_proj, total_square = sums((first, image), (second, image), (image, image))
    coef_cross = total_cross / count
    coef_second = total_proj / count
    rest = image - spread(coef_cross) * first - spread(coef_second) * second
    norm_second = jnp.sqrt(
        total_square / count - coef_cross * coef_cross - coef_second * coef_second + EPSILON
    )
    third = (rest / spread(norm_second)).reshape(shape)
    hess = jnp.stack(
        [scale_start, coef_first, norm_first, coef_cross, coef_second, norm_second], axis=1
    )
    return (third, hess)


def solution(mesh):
    placed = (
        P("gx", "gy", None, None, None),
        P("gx", "gy", None),
        P("gx", "gy"),
        P(),
        P(),
        P(),
        P(),
    )
    return jax.shard_map(
        body,
        mesh=mesh,
        in_specs=placed,
        out_specs=(P("gx", "gy", None, None, None), P()),
        check_vma=False,
    )
```

```python
import functools

import jax
import jax.numpy as jnp
from jax import lax
from jax.experimental import pallas as pl
from jax.experimental.pallas import tpu as pltpu
from jax.sharding import PartitionSpec as P

EPSILON = 1e-06
NEAR_BASE = ((0, 0), (1, -1), (1, 0), (1, 1), (0, 1))
AROUND = [(a, b) for a in (-1, 0, 1) for b in (-1, 0, 1)]
COMPASS = [d for d in AROUND if d != (0, 0)]
MESH = pl.DeviceIdType.MESH
VMEM = pl.BlockSpec(memory_space=pltpu.VMEM)


def near_lookup():
    table = {}
    for slot, (a, b) in enumerate(NEAR_BASE):
        table[(a, b)] = (slot, False)
        if (a, b) != (0, 0):
            table[(-a, -b)] = (slot, True)
    return table


def far_lookup():
    base = [
        (a, b)
        for a in range(-3, 4)
        for b in range(-3, 4)
        if max(abs(a), abs(b)) >= 2 and (a > 0 or (a == 0 and b > 0))
    ]
    table = {}
    for slot, (a, b) in enumerate(base):
        table[(a, b)] = (slot, False)
        table[(-a, -b)] = (slot, True)
    return table


def halves(values):
    high = values.astype(jnp.bfloat16)
    return high, (values - high.astype(jnp.float32)).astype(jnp.bfloat16)


def far_kernel(coupling, high, low):
    table = far_lookup()
    rank = coupling.shape[2]
    children = [(c, e) for c in (0, 1) for e in (0, 1)]
    empty = jnp.zeros((rank, rank), jnp.float32)
    row = 0
    for px, py in AROUND:
        for c, e in children:
            line = []
            for tc, te in children:
                found = table.get((2 * px + c - tc, 2 * py + e - te))
                if found is None:
                    line.append(empty)
                else:
                    block = coupling[0, found[0]]
                    line.append(block.T if found[1] else block)
            high[0, row : row + rank, :], low[0, row : row + rank, :] = halves(
                jnp.concatenate(line, axis=1)
            )
            row += rank


def far_matrices(coupling):
    levels, slots, rank, _ = coupling.shape
    spec = pl.BlockSpec((1, 36 * rank, 4 * rank), lambda i: (i, 0, 0))
    shape = jax.ShapeDtypeStruct((levels, 36 * rank, 4 * rank), jnp.bfloat16)
    return pl.pallas_call(
        far_kernel,
        grid=(levels,),
        in_specs=[pl.BlockSpec((1, slots, rank, rank), lambda i: (i, 0, 0, 0))],
        out_specs=[spec, spec],
        out_shape=[shape, shape],
    )(coupling)


def place(index, size_y):
    return {"gx": index // size_y, "gy": index % size_y}


def greet_all(size_x, size_y):
    total = size_x * size_y
    me = lax.axis_index("gx") * size_y + lax.axis_index("gy")
    barrier = pltpu.get_barrier_semaphore()

    def greet(step, carry):
        other = (me + step) % total
        pl.semaphore_signal(
            barrier, inc=1, device_id=place(other, size_y), device_id_type=MESH
        )
        return carry

    lax.fori_loop(1, total, greet, 0)
    pl.semaphore_wait(barrier, total - 1)


def gather_copy(source, target, send, receive, step, size_x, size_y):
    total = size_x * size_y
    me = lax.axis_index("gx") * size_y + lax.axis_index("gy")
    other = (me + step) % total
    return pltpu.make_async_remote_copy(
        src_ref=source,
        dst_ref=target.at[me],
        send_sem=send.at[step],
        recv_sem=receive.at[step],
        device_id=place(other, size_y),
        device_id_type=MESH,
    )


def sum_kernel(size_x, size_y, part, out, slots, send, receive):
    total = size_x * size_y
    me = lax.axis_index("gx") * size_y + lax.axis_index("gy")
    greet_all(size_x, size_y)

    def begin(step, carry):
        gather_copy(part, slots, send, receive, step, size_x, size_y).start()
        return carry

    def finish(step, carry):
        source = (me + total - step) % total
        pltpu.make_async_remote_copy(
            src_ref=part,
            dst_ref=slots.at[source],
            send_sem=send.at[step],
            recv_sem=receive.at[step],
            device_id=place((me + step) % total, size_y),
            device_id_type=MESH,
        ).wait()
        return carry

    lax.fori_loop(1, total, begin, 0)
    slots[me] = part[...]
    lax.fori_loop(1, total, finish, 0)
    out[...] = jnp.sum(slots[...], axis=0)


def sum_all(values, size_x, size_y):
    rows, columns = values.shape
    part = jnp.pad(values, ((0, 8 - rows), (0, 128 - columns)))
    total = size_x * size_y
    summed = pl.pallas_call(
        functools.partial(sum_kernel, size_x, size_y),
        in_specs=[VMEM],
        out_specs=VMEM,
        out_shape=jax.ShapeDtypeStruct((8, 128), jnp.float32),
        scratch_shapes=[
            pltpu.VMEM((total, 8, 128), jnp.float32),
            pltpu.SemaphoreType.DMA((total,)),
            pltpu.SemaphoreType.DMA((total,)),
        ],
        compiler_params=pltpu.CompilerParams(collective_id=0, has_side_effects=True),
    )(part)
    return summed[:rows, :columns]


def strip(move, length):
    if move > 0:
        return pl.ds(length, 1), pl.ds(0, 1)
    if move < 0:
        return pl.ds(1, 1), pl.ds(length + 1, 1)
    return pl.ds(1, length), pl.ds(1, length)


def stacked(values):
    high = values.astype(jnp.bfloat16).astype(jnp.float32)
    return jnp.concatenate([high, values - high], axis=0).astype(jnp.bfloat16)


def product(left, right, across=1):
    return lax.dot_general(
        left, right, (((1,), (1 - across,)), ((), ())), preferred_element_type=jnp.float32
    )


def times(values, high, low, across=1):
    both = stacked(values)
    total = product(both, high, across) + product(both, low, across)
    rows = values.shape[0]
    return total[:rows] + total[rows:]


def group(boxes, size_x, size_y):
    rows = []
    for x in range(0, size_x, 2):
        for y in range(0, size_y, 2):
            four = [(x + c) * size_y + y + e for c in (0, 1) for e in (0, 1)]
            rows.append(jnp.concatenate([boxes[8 * i : 8 * i + 8] for i in four], axis=1))
    return rows


def ungroup(parents, size_x, size_y):
    rank = parents.shape[1] // 4
    rows = []
    for x in range(2 * size_x):
        for y in range(2 * size_y):
            i = (x // 2) * size_y + y // 2
            k = 2 * (x % 2) + y % 2
            rows.append(parents[8 * i : 8 * i + 8, k * rank : (k + 1) * rank])
    return jnp.concatenate(rows, axis=0)


def clear_rim(out):
    long_x, long_y = out.shape[0], out.shape[1]
    line_x = jnp.zeros((1,) + out.shape[1:], out.dtype)
    line_y = jnp.zeros((long_x, 1) + out.shape[2:], out.dtype)
    out[0:1] = line_x
    out[long_x - 1 : long_x] = line_x
    out[:, 0:1] = line_y
    out[:, long_y - 1 : long_y] = line_y


def operate_kernel(size_x, size_y, inner, *refs):
    source, near, basis, lifts, far_high, far_low, out = refs[:7]
    padded = refs[7]
    pyramid = refs[8 : 8 + inner]
    rest = refs[8 + inner :]
    coarse = far_high.shape[0] - inner
    tops = rest[:coarse]
    mine, gathered, shifted, total, send, receive, gather_send, gather_receive = rest[coarse:]
    side = source.shape[0]
    width = source.shape[3]
    rank = basis.shape[1]
    devices = size_x * size_y
    me_x, me_y = lax.axis_index("gx"), lax.axis_index("gy")
    me = me_x * size_y + me_y
    ways = range(len(COMPASS))
    bands = (padded,) + tuple(pyramid)

    for band in bands + tuple(tops):
        clear_rim(band)
    padded[1 : 1 + side, 1 : 1 + side] = source[...]
    greet_all(size_x, size_y)

    def copy_of(number, way):
        move_x, move_y = COMPASS[way]
        band = bands[number]
        from_x, to_x = strip(move_x, band.shape[0] - 2)
        from_y, to_y = strip(move_y, band.shape[1] - 2)
        return pltpu.make_async_remote_copy(
            src_ref=band.at[from_x, from_y],
            dst_ref=band.at[to_x, to_y],
            send_sem=send.at[number, way],
            recv_sem=receive.at[number, way],
            device_id={"gx": me_x + move_x, "gy": me_y + move_y},
            device_id_type=MESH,
        )

    def inside(place_x, place_y):
        return (place_x >= 0) & (place_x < size_x) & (place_y >= 0) & (place_y < size_y)

    def start_bands(numbers):
        for way in ways:
            move_x, move_y = COMPASS[way]

            @pl.when(inside(me_x + move_x, me_y + move_y))
            def _(way=way):
                for number in numbers:
                    copy_of(number, way).start()

    def finish_bands(numbers):
        for way in ways:
            move_x, move_y = COMPASS[way]

            @pl.when(inside(me_x + move_x, me_y + move_y))
            def _(way=way):
                for number in numbers:
                    copy_of(number, way).wait_send()

            @pl.when(inside(me_x - move_x, me_y - move_y))
            def _(way=way):
                for number in numbers:
                    copy_of(number, way).wait_recv()

    start_bands((0,))

    flat = source[...].astype(jnp.float32).reshape(side * side * 8, width).astype(jnp.bfloat16)
    level = product(flat, basis[...])
    span = side
    for depth in range(inner):
        parents = group(level, span, span)
        span //= 2
        for i, parent in enumerate(parents):
            pyramid[depth][1 + i // span, 1 + i % span] = parent
        high, low = halves(lifts[depth])
        level = times(jnp.concatenate(parents, axis=0), high, low)
    mine[...] = level
    gathered[me] = level
    start_bands(range(1, inner + 1))

    def begin(step, carry):
        gather_copy(mine, gathered, gather_send, gather_receive, step, size_x, size_y).start()
        return carry

    lax.fori_loop(1, devices, begin, 0)

    finish_bands((0,))
    for b in range(3):
        shifted[b] = (
            padded[:, b : b + side]
            .astype(jnp.float32)
            .reshape((side + 2) * side * 8, width)
            .astype(jnp.bfloat16)
        )
    rows = side * side * 8
    table = near_lookup()
    chunk = 256 if width % 256 == 0 else 128

    def near_columns(index, carry):
        columns = pl.ds(pl.multiple_of(index * chunk, chunk), chunk)
        value = jnp.zeros((rows, chunk), jnp.float32)
        for a, b in AROUND:
            slot, flipped = table[(a, b)]
            piece = shifted[1 + b, (1 + a) * side * 8 : (1 + a) * side * 8 + rows]
            if flipped:
                value = value + product(piece, near[slot, columns, :], 0)
            else:
                value = value + product(piece, near[slot, :, columns])
        total[:, columns] = value
        return carry

    lax.fori_loop(0, width // chunk, near_columns, 0)
    finish_bands(range(1, inner + 1))

    def finish(step, carry):
        other = (me + devices - step) % devices
        pltpu.make_async_remote_copy(
            src_ref=mine,
            dst_ref=gathered.at[other],
            send_sem=gather_send.at[step],
            recv_sem=gather_receive.at[step],
            device_id=place((me + step) % devices, size_y),
            device_id_type=MESH,
        ).wait()
        return carry

    lax.fori_loop(1, devices, finish, 0)

    def couple(depth, window):
        value = None
        for k, (a, b) in enumerate(AROUND):
            span_rows = slice(4 * rank * k, 4 * rank * (k + 1))
            term = times(window(a, b), far_high[depth, span_rows], far_low[depth, span_rows])
            value = term if value is None else value + term
        return value

    across, along = size_x, size_y
    boxes = gathered[...].reshape(devices * 8, rank)
    for step in range(coarse):
        parents = group(boxes, across, along)
        across, along = across // 2, along // 2
        for i, parent in enumerate(parents):
            tops[step][1 + i // along, 1 + i % along] = parent
        if step < coarse - 1:
            high, low = halves(lifts[inner + step])
            boxes = times(jnp.concatenate(parents, axis=0), high, low)
    down = None
    for step in range(coarse - 1, -1, -1):
        near_x, near_y = me_x >> step + 1, me_y >> step + 1
        value = couple(
            inner + step, lambda a, b: tops[step][near_x + (1 + a), near_y + (1 + b)]
        )
        if down is not None:
            high, low = halves(lifts[inner + step])
            value = value + times(down, high, low, 0)
        child = 2 * (me_x >> step & 1) + (me_y >> step & 1)
        down = jnp.zeros((8, rank), jnp.float32)
        for i in range(4):
            down = jnp.where(child == i, value[:, i * rank : (i + 1) * rank], down)

    span = 1
    for depth in range(inner - 1, -1, -1):
        band = pyramid[depth]
        value = couple(
            depth,
            lambda a, b: band[1 + a : 1 + a + span, 1 + b : 1 + b + span].reshape(
                span * span * 8, 4 * rank
            ),
        )
        high, low = halves(lifts[depth])
        value = value + times(down, high, low, 0)
        down = ungroup(value, span, span)
        span *= 2
    spread_down = product(stacked(down), basis[...], 0)
    out[...] = (total[...] + spread_down[:rows] + spread_down[rows:]).reshape(out.shape)


def apply(source, near, basis, lifts, far_high, far_low, size_x, size_y):
    side, _, _, width = source.shape
    rank = basis.shape[1]
    inner = side.bit_length() - 1
    coarse = far_high.shape[0] - inner
    devices = size_x * size_y
    halos = inner + 1
    scratch = [pltpu.VMEM((side + 2, side + 2, 8, width), jnp.bfloat16)]
    for depth in range(inner):
        span = (side >> depth + 1) + 2
        scratch.append(pltpu.VMEM((span, span, 8, 4 * rank), jnp.float32))
    for step in range(coarse):
        grid = ((size_x >> step + 1) + 2, (size_y >> step + 1) + 2)
        scratch.append(pltpu.VMEM(grid + (8, 4 * rank), jnp.float32))
    scratch += [
        pltpu.VMEM((8, rank), jnp.float32),
        pltpu.VMEM((devices, 8, rank), jnp.float32),
        pltpu.VMEM((3, (side + 2) * side * 8, width), jnp.bfloat16),
        pltpu.VMEM((side * side * 8, width), jnp.float32),
        pltpu.SemaphoreType.DMA((halos, len(COMPASS))),
        pltpu.SemaphoreType.DMA((halos, len(COMPASS))),
        pltpu.SemaphoreType.DMA((devices,)),
        pltpu.SemaphoreType.DMA((devices,)),
    ]
    return pl.pallas_call(
        functools.partial(operate_kernel, size_x, size_y, inner),
        in_specs=[VMEM] * 6,
        out_specs=VMEM,
        out_shape=jax.ShapeDtypeStruct(source.shape, jnp.float32),
        scratch_shapes=scratch,
        compiler_params=pltpu.CompilerParams(collective_id=1, has_side_effects=True),
    )(source, near, basis, lifts, far_high, far_low)


def body(rhs, contrast, occupied, near, basis, transfer, coupling):
    shape = rhs.shape
    side, _, fields, parts, voxels = shape
    width = parts * voxels
    rank = basis.shape[1]
    levels = transfer.shape[0] + 1
    devices_x = lax.axis_size("gx")
    devices_y = lax.axis_size("gy")
    count = float(side * side * devices_x * devices_y * width)
    rhs = rhs.reshape(side, side, fields, width)
    weight = occupied.astype(jnp.float32)[:, :, None] * contrast
    weight = jnp.tile(weight, (1, 1, parts))[:, :, None, :]
    lifts = transfer.reshape(levels - 1, 4 * rank, rank)
    far_high, far_low = far_matrices(coupling)

    def operate(field):
        source = (weight * field).astype(jnp.bfloat16)
        source = jnp.pad(source, ((0, 0), (0, 0), (0, 8 - fields), (0, 0)))
        moved = apply(source, near, basis, lifts, far_high, far_low, devices_x, devices_y)
        return field + moved[:, :, :fields]

    def local_sum(one, other):
        return jnp.sum(one * other, axis=(0, 1, 3))

    def sums(*pairs):
        values = jnp.stack([local_sum(one, other) for one, other in pairs], axis=1)
        summed = sum_all(values, devices_x, devices_y)
        return [summed[:, i] for i in range(len(pairs))]

    def spread(values):
        return values[None, None, :, None]

    (square,) = sums((rhs, rhs))
    scale_start = jnp.sqrt(square / count + EPSILON)
    first = rhs / spread(scale_start)
    image = operate(first)
    total_proj, total_square = sums((first, image), (image, image))
    coef_first = total_proj / count
    norm_first = jnp.sqrt(total_square / count - coef_first * coef_first + EPSILON)
    second = (image - spread(coef_first) * first) / spread(norm_first)
    image = operate(second)
    total_cross, total_proj, total_square = sums((first, image), (second, image), (image, image))
    coef_cross = total_cross / count
    coef_second = total_proj / count
    rest = image - spread(coef_cross) * first - spread(coef_second) * second
    norm_second = jnp.sqrt(
        total_square / count - coef_cross * coef_cross - coef_second * coef_second + EPSILON
    )
    third = (rest / spread(norm_second)).reshape(shape)
    hess = jnp.stack(
        [scale_start, coef_first, norm_first, coef_cross, coef_second, norm_second], axis=1
    )
    return (third, hess)


def solution(mesh):
    placed = (
        P("gx", "gy", None, None, None),
        P("gx", "gy", None),
        P("gx", "gy"),
        P(),
        P(),
        P(),
        P(),
    )
    return jax.shard_map(
        body,
        mesh=mesh,
        in_specs=placed,
        out_specs=(P("gx", "gy", None, None, None), P()),
        check_vma=False,
    )
```

```python
import functools

import jax
import jax.numpy as jnp
from jax import lax
from jax.experimental import pallas as pl
from jax.experimental.pallas import tpu as pltpu
from jax.sharding import PartitionSpec as P

EPSILON = 1e-06
NEAR_BASE = ((0, 0), (1, -1), (1, 0), (1, 1), (0, 1))
AROUND = [(a, b) for a in (-1, 0, 1) for b in (-1, 0, 1)]
COMPASS = [d for d in AROUND if d != (0, 0)]
MESH = pl.DeviceIdType.MESH
VMEM = pl.BlockSpec(memory_space=pltpu.VMEM)


def near_lookup():
    table = {}
    for slot, (a, b) in enumerate(NEAR_BASE):
        table[(a, b)] = (slot, False)
        if (a, b) != (0, 0):
            table[(-a, -b)] = (slot, True)
    return table


def far_lookup():
    base = [
        (a, b)
        for a in range(-3, 4)
        for b in range(-3, 4)
        if max(abs(a), abs(b)) >= 2 and (a > 0 or (a == 0 and b > 0))
    ]
    table = {}
    for slot, (a, b) in enumerate(base):
        table[(a, b)] = (slot, False)
        table[(-a, -b)] = (slot, True)
    return table


def halves(values):
    high = values.astype(jnp.bfloat16)
    return high, (values - high.astype(jnp.float32)).astype(jnp.bfloat16)


def far_level(depth, coupling, high, low):
    table = far_lookup()
    rank = coupling.shape[2]
    children = [(c, e) for c in (0, 1) for e in (0, 1)]
    empty = jnp.zeros((rank, rank), jnp.float32)
    row = 0
    for px, py in AROUND:
        for c, e in children:
            line = []
            for tc, te in children:
                found = table.get((2 * px + c - tc, 2 * py + e - te))
                if found is None:
                    line.append(empty)
                else:
                    block = coupling[depth, found[0]]
                    line.append(block.T if found[1] else block)
            high[depth, row : row + rank, :], low[depth, row : row + rank, :] = halves(
                jnp.concatenate(line, axis=1)
            )
            row += rank


def place(index, size_y):
    return {"gx": index // size_y, "gy": index % size_y}


def greet_all(size_x, size_y):
    total = size_x * size_y
    me = lax.axis_index("gx") * size_y + lax.axis_index("gy")
    barrier = pltpu.get_barrier_semaphore()

    def greet(step, carry):
        other = (me + step) % total
        pl.semaphore_signal(
            barrier, inc=1, device_id=place(other, size_y), device_id_type=MESH
        )
        return carry

    lax.fori_loop(1, total, greet, 0)


def await_greetings(size_x, size_y):
    pl.semaphore_wait(pltpu.get_barrier_semaphore(), size_x * size_y - 1)


def gather_copy(source, target, send, receive, step, size_x, size_y):
    total = size_x * size_y
    me = lax.axis_index("gx") * size_y + lax.axis_index("gy")
    other = (me + step) % total
    return pltpu.make_async_remote_copy(
        src_ref=source,
        dst_ref=target.at[me],
        send_sem=send.at[step],
        recv_sem=receive.at[step],
        device_id=place(other, size_y),
        device_id_type=MESH,
    )


def strip(move, length):
    if move > 0:
        return pl.ds(length, 1), pl.ds(0, 1)
    if move < 0:
        return pl.ds(1, 1), pl.ds(length + 1, 1)
    return pl.ds(1, length), pl.ds(1, length)


def stacked(values):
    high = values.astype(jnp.bfloat16).astype(jnp.float32)
    return jnp.concatenate([high, values - high], axis=0).astype(jnp.bfloat16)


def product(left, right, across=1):
    return lax.dot_general(
        left, right, (((1,), (1 - across,)), ((), ())), preferred_element_type=jnp.float32
    )


def times(values, high, low, across=1):
    both = stacked(values)
    total = product(both, high, across) + product(both, low, across)
    rows = values.shape[0]
    return total[:rows] + total[rows:]


def group(boxes, size_x, size_y):
    rows = []
    for x in range(0, size_x, 2):
        for y in range(0, size_y, 2):
            four = [(x + c) * size_y + y + e for c in (0, 1) for e in (0, 1)]
            rows.append(jnp.concatenate([boxes[8 * i : 8 * i + 8] for i in four], axis=1))
    return rows


def ungroup(parents, size_x, size_y):
    rank = parents.shape[1] // 4
    rows = []
    for x in range(2 * size_x):
        for y in range(2 * size_y):
            i = (x // 2) * size_y + y // 2
            k = 2 * (x % 2) + y % 2
            rows.append(parents[8 * i : 8 * i + 8, k * rank : (k + 1) * rank])
    return jnp.concatenate(rows, axis=0)


def clear_rim(out):
    long_x, long_y = out.shape[0], out.shape[1]
    line_x = jnp.zeros((1,) + out.shape[1:], out.dtype)
    line_y = jnp.zeros((long_x, 1) + out.shape[2:], out.dtype)
    out[0:1] = line_x
    out[long_x - 1 : long_x] = line_x
    out[:, 0:1] = line_y
    out[:, long_y - 1 : long_y] = line_y


def krylov_kernel(size_x, size_y, inner, count, *refs):
    rhs, weight, near_far_away, basis, lifts, coupling, third, hess = refs[:8]
    near, far_high, far_low, first, second, source = refs[8:14]
    padded = refs[14]
    pyramid = refs[15 : 15 + inner]
    rest = refs[15 + inner :]
    coarse = coupling.shape[0] - inner
    tops = rest[:coarse]
    mine, gathered, shifted, total, parts, slots = rest[coarse : coarse + 6]
    send, receive, gather_send, gather_receive, sum_send, sum_receive, load = rest[coarse + 6 :]
    side = source.shape[0]
    width = source.shape[3]
    rank = basis.shape[1]
    devices = size_x * size_y
    me_x, me_y = lax.axis_index("gx"), lax.axis_index("gy")
    me = me_x * size_y + me_y
    ways = range(len(COMPASS))
    bands = (padded,) + tuple(pyramid)
    rows = side * side * 8
    lane = lax.broadcasted_iota(jnp.int32, (8, 128), 1)

    def tile_of(columns):
        tile = jnp.zeros((8, 128), jnp.float32)
        for i, column in enumerate(columns):
            tile = jnp.where(lane == i, column, tile)
        return tile

    def start_sums(number, sums):
        tile = tile_of([jnp.sum(value, axis=1, keepdims=True) for value in sums])
        parts[number] = tile
        slots[number, me] = tile

        def begin(step, carry):
            gather_copy(
                parts.at[number],
                slots.at[number],
                sum_send.at[number],
                sum_receive.at[number],
                step,
                size_x,
                size_y,
            ).start()
            return carry

        lax.fori_loop(1, devices, begin, 0)

    def finish_gather(piece, target, sent, received):
        def finish(step, carry):
            other = (me + devices - step) % devices
            pltpu.make_async_remote_copy(
                src_ref=piece,
                dst_ref=target.at[other],
                send_sem=sent.at[step],
                recv_sem=received.at[step],
                device_id=place((me + step) % devices, size_y),
                device_id_type=MESH,
            ).wait()
            return carry

        lax.fori_loop(1, devices, finish, 0)

    def finish_sums(number, amount):
        finish_gather(
            parts.at[number], slots.at[number], sum_send.at[number], sum_receive.at[number]
        )
        tile = jnp.sum(slots[number], axis=0) / count
        return [tile[:, i : i + 1] for i in range(amount)]

    def rows_sum(value):
        return jnp.sum(value, axis=0)

    def sweep(amount, work):
        def one(x, sums):
            return tuple(old + new for old, new in zip(sums, work(x)))

        return lax.fori_loop(0, side, one, (jnp.zeros((8, width), jnp.float32),) * amount)

    near_copy = pltpu.make_async_copy(near_far_away, near, load.at[0])
    near_copy.start()
    for band in bands + tuple(tops):
        clear_rim(band)
    greet_all(size_x, size_y)
    sums = sweep(1, lambda x: (rows_sum(rhs[x] * rhs[x]),))
    await_greetings(size_x, size_y)
    start_sums(0, sums)

    def build(depth, carry):
        far_level(depth, coupling, far_high, far_low)
        return carry

    lax.fori_loop(0, coupling.shape[0], build, 0)
    (square,) = finish_sums(0, 1)
    beta = jnp.sqrt(square + EPSILON)

    def copy_of(number, way):
        move_x, move_y = COMPASS[way]
        band = bands[number]
        from_x, to_x = strip(move_x, band.shape[0] - 2)
        from_y, to_y = strip(move_y, band.shape[1] - 2)
        return pltpu.make_async_remote_copy(
            src_ref=band.at[from_x, from_y],
            dst_ref=band.at[to_x, to_y],
            send_sem=send.at[number, way],
            recv_sem=receive.at[number, way],
            device_id={"gx": me_x + move_x, "gy": me_y + move_y},
            device_id_type=MESH,
        )

    def inside(place_x, place_y):
        return (place_x >= 0) & (place_x < size_x) & (place_y >= 0) & (place_y < size_y)

    def start_bands(numbers):
        for way in ways:
            move_x, move_y = COMPASS[way]

            @pl.when(inside(me_x + move_x, me_y + move_y))
            def _(way=way):
                for number in numbers:
                    copy_of(number, way).start()

    def finish_bands(numbers):
        for way in ways:
            move_x, move_y = COMPASS[way]

            @pl.when(inside(me_x + move_x, me_y + move_y))
            def _(way=way):
                for number in numbers:
                    copy_of(number, way).wait_send()

            @pl.when(inside(me_x - move_x, me_y - move_y))
            def _(way=way):
                for number in numbers:
                    copy_of(number, way).wait_recv()

    def operate():
        padded[1 : 1 + side, 1 : 1 + side] = source[...]
        start_bands((0,))

        flat = source[...].astype(jnp.float32).reshape(side * side * 8, width).astype(jnp.bfloat16)
        level = product(flat, basis[...])
        span = side
        for depth in range(inner):
            parents = group(level, span, span)
            span //= 2
            for i, parent in enumerate(parents):
                pyramid[depth][1 + i // span, 1 + i % span] = parent
            high, low = halves(lifts[depth])
            level = times(jnp.concatenate(parents, axis=0), high, low)
        mine[...] = level
        gathered[me] = level
        start_bands(range(1, inner + 1))

        def begin(step, carry):
            gather_copy(mine, gathered, gather_send, gather_receive, step, size_x, size_y).start()
            return carry

        lax.fori_loop(1, devices, begin, 0)

        finish_bands((0,))
        for b in range(3):
            shifted[b] = (
                padded[:, b : b + side]
                .astype(jnp.float32)
                .reshape((side + 2) * side * 8, width)
                .astype(jnp.bfloat16)
            )
        table = near_lookup()
        chunk = 256 if width % 256 == 0 else 128

        def near_columns(index, carry):
            columns = pl.ds(pl.multiple_of(index * chunk, chunk), chunk)
            value = jnp.zeros((rows, chunk), jnp.float32)
            for a, b in AROUND:
                slot, flipped = table[(a, b)]
                piece = shifted[1 + b, (1 + a) * side * 8 : (1 + a) * side * 8 + rows]
                if flipped:
                    value = value + product(piece, near[slot, columns, :], 0)
                else:
                    value = value + product(piece, near[slot, :, columns])
            total[:, columns] = value
            return carry

        lax.fori_loop(0, width // chunk, near_columns, 0)
        finish_bands(range(1, inner + 1))

        finish_gather(mine, gathered, gather_send, gather_receive)

        def couple(depth, window):
            value = None
            for k, (a, b) in enumerate(AROUND):
                span_rows = slice(4 * rank * k, 4 * rank * (k + 1))
                term = times(window(a, b), far_high[depth, span_rows], far_low[depth, span_rows])
                value = term if value is None else value + term
            return value

        across, along = size_x, size_y
        boxes = gathered[...].reshape(devices * 8, rank)
        for step in range(coarse):
            parents = group(boxes, across, along)
            across, along = across // 2, along // 2
            for i, parent in enumerate(parents):
                tops[step][1 + i // along, 1 + i % along] = parent
            if step < coarse - 1:
                high, low = halves(lifts[inner + step])
                boxes = times(jnp.concatenate(parents, axis=0), high, low)
        down = None
        for step in range(coarse - 1, -1, -1):
            near_x, near_y = me_x >> step + 1, me_y >> step + 1
            value = couple(
                inner + step, lambda a, b: tops[step][near_x + (1 + a), near_y + (1 + b)]
            )
            if down is not None:
                high, low = halves(lifts[inner + step])
                value = value + times(down, high, low, 0)
            child = 2 * (me_x >> step & 1) + (me_y >> step & 1)
            down = jnp.zeros((8, rank), jnp.float32)
            for i in range(4):
                down = jnp.where(child == i, value[:, i * rank : (i + 1) * rank], down)

        span = 1
        for depth in range(inner - 1, -1, -1):
            band = pyramid[depth]
            value = couple(
                depth,
                lambda a, b: band[1 + a : 1 + a + span, 1 + b : 1 + b + span].reshape(
                    span * span * 8, 4 * rank
                ),
            )
            high, low = halves(lifts[depth])
            value = value + times(down, high, low, 0)
            down = ungroup(value, span, span)
            span *= 2
        spread_down = product(stacked(down), basis[...], 0)
        total[...] = total[...] + spread_down[:rows] + spread_down[rows:]

    boxes_of = side * 8

    def image_of(x, field):
        return field[x] + total[pl.ds(pl.multiple_of(x * boxes_of, 8), boxes_of)].reshape(
            side, 8, width
        )

    def set_first(x, carry):
        value = rhs[x] * inverse
        first[x] = value
        source[x] = (weight[x] * value).astype(jnp.bfloat16)
        return carry

    inverse = 1.0 / beta
    lax.fori_loop(0, side, set_first, 0)
    near_copy.wait()
    operate()

    def first_sums(x):
        value, image = first[x], image_of(x, first)
        second[x] = image
        return rows_sum(value * image), rows_sum(image * image)

    start_sums(1, sweep(2, first_sums))
    h11, square = finish_sums(1, 2)
    h21 = jnp.sqrt(square - h11 * h11 + EPSILON)
    inverse_second = 1.0 / h21

    def set_second(x, carry):
        value = (second[x] - h11 * first[x]) * inverse_second
        second[x] = value
        source[x] = (weight[x] * value).astype(jnp.bfloat16)
        return carry

    lax.fori_loop(0, side, set_second, 0)
    operate()

    def second_sums(x):
        image = image_of(x, second)
        third[x] = image
        return rows_sum(first[x] * image), rows_sum(second[x] * image), rows_sum(image * image)

    start_sums(2, sweep(3, second_sums))
    h12, h22, square = finish_sums(2, 3)
    h32 = jnp.sqrt(square - h12 * h12 - h22 * h22 + EPSILON)
    inverse_third = 1.0 / h32

    def set_third(x, carry):
        third[x] = (third[x] - h12 * first[x] - h22 * second[x]) * inverse_third
        return carry

    lax.fori_loop(0, side, set_third, 0)
    hess[...] = tile_of([beta, h11, h21, h12, h22, h32])


def krylov(rhs, weight, near, basis, lifts, coupling, count, size_x, size_y):
    side, _, _, width = rhs.shape
    rank = basis.shape[1]
    inner = side.bit_length() - 1
    levels = coupling.shape[0]
    coarse = levels - inner
    devices = size_x * size_y
    halos = inner + 1
    scratch = [
        pltpu.VMEM(near.shape, near.dtype),
        pltpu.VMEM((levels, 36 * rank, 4 * rank), jnp.bfloat16),
        pltpu.VMEM((levels, 36 * rank, 4 * rank), jnp.bfloat16),
        pltpu.VMEM(rhs.shape, jnp.float32),
        pltpu.VMEM(rhs.shape, jnp.float32),
        pltpu.VMEM(rhs.shape, jnp.bfloat16),
        pltpu.VMEM((side + 2, side + 2, 8, width), jnp.bfloat16),
    ]
    for depth in range(inner):
        span = (side >> depth + 1) + 2
        scratch.append(pltpu.VMEM((span, span, 8, 4 * rank), jnp.float32))
    for step in range(coarse):
        grid = ((size_x >> step + 1) + 2, (size_y >> step + 1) + 2)
        scratch.append(pltpu.VMEM(grid + (8, 4 * rank), jnp.float32))
    scratch += [
        pltpu.VMEM((8, rank), jnp.float32),
        pltpu.VMEM((devices, 8, rank), jnp.float32),
        pltpu.VMEM((3, (side + 2) * side * 8, width), jnp.bfloat16),
        pltpu.VMEM((side * side * 8, width), jnp.float32),
        pltpu.VMEM((3, 8, 128), jnp.float32),
        pltpu.VMEM((3, devices, 8, 128), jnp.float32),
        pltpu.SemaphoreType.DMA((halos, len(COMPASS))),
        pltpu.SemaphoreType.DMA((halos, len(COMPASS))),
        pltpu.SemaphoreType.DMA((devices,)),
        pltpu.SemaphoreType.DMA((devices,)),
        pltpu.SemaphoreType.DMA((3, devices)),
        pltpu.SemaphoreType.DMA((3, devices)),
        pltpu.SemaphoreType.DMA((1,)),
    ]
    return pl.pallas_call(
        functools.partial(krylov_kernel, size_x, size_y, inner, count),
        in_specs=[VMEM, VMEM, pl.BlockSpec(memory_space=pl.ANY), VMEM, VMEM, VMEM],
        out_specs=[VMEM, VMEM],
        out_shape=[
            jax.ShapeDtypeStruct(rhs.shape, jnp.float32),
            jax.ShapeDtypeStruct((8, 128), jnp.float32),
        ],
        scratch_shapes=scratch,
        compiler_params=pltpu.CompilerParams(collective_id=0, has_side_effects=True),
    )(rhs, weight, near, basis, lifts, coupling)


def body(rhs, contrast, occupied, near, basis, transfer, coupling):
    shape = rhs.shape
    side, _, fields, parts, voxels = shape
    width = parts * voxels
    rank = basis.shape[1]
    devices_x = lax.axis_size("gx")
    devices_y = lax.axis_size("gy")
    count = float(side * side * devices_x * devices_y * width)
    flat = rhs.reshape(side, side, fields, width)
    flat = jnp.pad(flat, ((0, 0), (0, 0), (0, 8 - fields), (0, 0)))
    weight = occupied.astype(jnp.float32)[:, :, None] * contrast
    weight = jnp.tile(weight, (1, 1, parts))[:, :, None, :]
    lifts = transfer.reshape(transfer.shape[0], 4 * rank, rank)
    third, hess = krylov(
        flat, weight, near, basis, lifts, coupling, count, devices_x, devices_y
    )
    return (third[:, :, :fields].reshape(shape), hess[:fields, :6])


def solution(mesh):
    placed = (
        P("gx", "gy", None, None, None),
        P("gx", "gy", None),
        P("gx", "gy"),
        P(),
        P(),
        P(),
        P(),
    )
    return jax.shard_map(
        body,
        mesh=mesh,
        in_specs=placed,
        out_specs=(P("gx", "gy", None, None, None), P()),
        check_vma=False,
    )
```

```python
import functools

import jax
import jax.numpy as jnp
from jax import lax
from jax.experimental import pallas as pl
from jax.experimental.pallas import tpu as pltpu
from jax.sharding import PartitionSpec as P

EPSILON = 1e-06
NEAR_BASE = ((0, 0), (1, -1), (1, 0), (1, 1), (0, 1))
AROUND = [(a, b) for a in (-1, 0, 1) for b in (-1, 0, 1)]
COMPASS = [d for d in AROUND if d != (0, 0)]
MESH = pl.DeviceIdType.MESH
VMEM = pl.BlockSpec(memory_space=pltpu.VMEM)


def near_lookup():
    table = {}
    for slot, (a, b) in enumerate(NEAR_BASE):
        table[(a, b)] = (slot, False)
        if (a, b) != (0, 0):
            table[(-a, -b)] = (slot, True)
    return table


def far_lookup():
    base = [
        (a, b)
        for a in range(-3, 4)
        for b in range(-3, 4)
        if max(abs(a), abs(b)) >= 2 and (a > 0 or (a == 0 and b > 0))
    ]
    table = {}
    for slot, (a, b) in enumerate(base):
        table[(a, b)] = (slot, False)
        table[(-a, -b)] = (slot, True)
    return table


def halves(values):
    high = values.astype(jnp.bfloat16)
    return high, (values - high.astype(jnp.float32)).astype(jnp.bfloat16)


def far_level(depth, coupling, high, low):
    table = far_lookup()
    rank = coupling.shape[2]
    children = [(c, e) for c in (0, 1) for e in (0, 1)]
    empty = jnp.zeros((rank, rank), jnp.float32)
    row = 0
    for px, py in AROUND:
        for c, e in children:
            line = []
            for tc, te in children:
                found = table.get((2 * px + c - tc, 2 * py + e - te))
                if found is None:
                    line.append(empty)
                else:
                    block = coupling[depth, found[0]]
                    line.append(block.T if found[1] else block)
            high[depth, row : row + rank, :], low[depth, row : row + rank, :] = halves(
                jnp.concatenate(line, axis=1)
            )
            row += rank


def place(index, size_y):
    return {"gx": index // size_y, "gy": index % size_y}


def greet_all(size_x, size_y):
    total = size_x * size_y
    me = lax.axis_index("gx") * size_y + lax.axis_index("gy")
    barrier = pltpu.get_barrier_semaphore()

    def greet(step, carry):
        other = (me + step) % total
        pl.semaphore_signal(
            barrier, inc=1, device_id=place(other, size_y), device_id_type=MESH
        )
        return carry

    lax.fori_loop(1, total, greet, 0)


def await_greetings(size_x, size_y):
    pl.semaphore_wait(pltpu.get_barrier_semaphore(), size_x * size_y - 1)


def gather_copy(source, target, send, receive, step, size_x, size_y):
    total = size_x * size_y
    me = lax.axis_index("gx") * size_y + lax.axis_index("gy")
    other = (me + step) % total
    return pltpu.make_async_remote_copy(
        src_ref=source,
        dst_ref=target.at[me],
        send_sem=send.at[step],
        recv_sem=receive.at[step],
        device_id=place(other, size_y),
        device_id_type=MESH,
    )


def strip(move, length):
    if move > 0:
        return pl.ds(length, 1), pl.ds(0, 1)
    if move < 0:
        return pl.ds(1, 1), pl.ds(length + 1, 1)
    return pl.ds(1, length), pl.ds(1, length)


def stacked(values):
    high = values.astype(jnp.bfloat16).astype(jnp.float32)
    return jnp.concatenate([high, values - high], axis=0).astype(jnp.bfloat16)


def product(left, right, across=1):
    return lax.dot_general(
        left, right, (((1,), (1 - across,)), ((), ())), preferred_element_type=jnp.float32
    )


def times(values, high, low, across=1):
    both = stacked(values)
    total = product(both, high, across) + product(both, low, across)
    rows = values.shape[0]
    return total[:rows] + total[rows:]


def group(boxes, size_x, size_y):
    rows = []
    for x in range(0, size_x, 2):
        for y in range(0, size_y, 2):
            four = [(x + c) * size_y + y + e for c in (0, 1) for e in (0, 1)]
            rows.append(jnp.concatenate([boxes[8 * i : 8 * i + 8] for i in four], axis=1))
    return rows


def ungroup(parents, size_x, size_y):
    rank = parents.shape[1] // 4
    rows = []
    for x in range(2 * size_x):
        for y in range(2 * size_y):
            i = (x // 2) * size_y + y // 2
            k = 2 * (x % 2) + y % 2
            rows.append(parents[8 * i : 8 * i + 8, k * rank : (k + 1) * rank])
    return jnp.concatenate(rows, axis=0)


def clear_rim(out):
    long_x, long_y = out.shape[0], out.shape[1]
    line_x = jnp.zeros((1,) + out.shape[1:], out.dtype)
    line_y = jnp.zeros((long_x, 1) + out.shape[2:], out.dtype)
    out[0:1] = line_x
    out[long_x - 1 : long_x] = line_x
    out[:, 0:1] = line_y
    out[:, long_y - 1 : long_y] = line_y


def krylov_kernel(size_x, size_y, inner, count, *refs):
    rhs, weight, near_far_away, basis, lifts, coupling, third, hess = refs[:8]
    near, far_high, far_low, first, second, source = refs[8:14]
    padded = refs[14]
    pyramid = refs[15 : 15 + inner]
    rest = refs[15 + inner :]
    coarse = coupling.shape[0] - inner
    tops = rest[:coarse]
    mine, gathered, shifted, total, parts, slots = rest[coarse : coarse + 6]
    send, receive, gather_send, gather_receive, sum_send, sum_receive, load = rest[coarse + 6 :]
    side = source.shape[0]
    width = source.shape[3]
    rank = basis.shape[0]
    devices = size_x * size_y
    me_x, me_y = lax.axis_index("gx"), lax.axis_index("gy")
    me = me_x * size_y + me_y
    ways = range(len(COMPASS))
    bands = (padded,) + tuple(pyramid)
    rows = side * side * 8
    lane = lax.broadcasted_iota(jnp.int32, (8, 128), 1)

    def tile_of(columns):
        tile = jnp.zeros((8, 128), jnp.float32)
        for i, column in enumerate(columns):
            tile = jnp.where(lane == i, column, tile)
        return tile

    def start_sums(number, sums):
        tile = tile_of([jnp.sum(value, axis=1, keepdims=True) for value in sums])
        parts[number] = tile
        slots[number, me] = tile

        def begin(step, carry):
            gather_copy(
                parts.at[number],
                slots.at[number],
                sum_send.at[number],
                sum_receive.at[number],
                step,
                size_x,
                size_y,
            ).start()
            return carry

        lax.fori_loop(1, devices, begin, 0)

    def finish_gather(piece, target, sent, received):
        def finish(step, carry):
            other = (me + devices - step) % devices
            pltpu.make_async_remote_copy(
                src_ref=piece,
                dst_ref=target.at[other],
                send_sem=sent.at[step],
                recv_sem=received.at[step],
                device_id=place((me + step) % devices, size_y),
                device_id_type=MESH,
            ).wait()
            return carry

        lax.fori_loop(1, devices, finish, 0)

    def finish_sums(number, amount):
        finish_gather(
            parts.at[number], slots.at[number], sum_send.at[number], sum_receive.at[number]
        )
        tile = jnp.sum(slots[number], axis=0) / count
        return [tile[:, i : i + 1] for i in range(amount)]

    def rows_sum(value):
        return jnp.sum(value, axis=0)

    def sweep(amount, work):
        def one(x, sums):
            return tuple(old + new for old, new in zip(sums, work(x)))

        return lax.fori_loop(0, side, one, (jnp.zeros((8, width), jnp.float32),) * amount)

    near_copy = pltpu.make_async_copy(near_far_away, near, load.at[0])
    near_copy.start()
    for band in bands + tuple(tops):
        clear_rim(band)
    greet_all(size_x, size_y)
    sums = sweep(1, lambda x: (rows_sum(rhs[x] * rhs[x]),))
    await_greetings(size_x, size_y)
    start_sums(0, sums)

    def build(depth, carry):
        far_level(depth, coupling, far_high, far_low)
        return carry

    lax.fori_loop(0, coupling.shape[0], build, 0)
    (square,) = finish_sums(0, 1)
    beta = jnp.sqrt(square + EPSILON)

    def copy_of(number, way):
        move_x, move_y = COMPASS[way]
        band = bands[number]
        from_x, to_x = strip(move_x, band.shape[0] - 2)
        from_y, to_y = strip(move_y, band.shape[1] - 2)
        return pltpu.make_async_remote_copy(
            src_ref=band.at[from_x, from_y],
            dst_ref=band.at[to_x, to_y],
            send_sem=send.at[number, way],
            recv_sem=receive.at[number, way],
            device_id={"gx": me_x + move_x, "gy": me_y + move_y},
            device_id_type=MESH,
        )

    def inside(place_x, place_y):
        return (place_x >= 0) & (place_x < size_x) & (place_y >= 0) & (place_y < size_y)

    def start_bands(numbers):
        for way in ways:
            move_x, move_y = COMPASS[way]

            @pl.when(inside(me_x + move_x, me_y + move_y))
            def _(way=way):
                for number in numbers:
                    copy_of(number, way).start()

    def finish_bands(numbers):
        for way in ways:
            move_x, move_y = COMPASS[way]

            @pl.when(inside(me_x + move_x, me_y + move_y))
            def _(way=way):
                for number in numbers:
                    copy_of(number, way).wait_send()

            @pl.when(inside(me_x - move_x, me_y - move_y))
            def _(way=way):
                for number in numbers:
                    copy_of(number, way).wait_recv()

    def operate():
        padded[1 : 1 + side, 1 : 1 + side] = source[...]
        start_bands((0,))

        flat = source[...].astype(jnp.float32).reshape(side * side * 8, width).astype(jnp.bfloat16)
        level = product(flat, basis[...], 0)
        span = side
        for depth in range(inner):
            parents = group(level, span, span)
            span //= 2
            for i, parent in enumerate(parents):
                pyramid[depth][1 + i // span, 1 + i % span] = parent
            high, low = halves(lifts[depth])
            level = times(jnp.concatenate(parents, axis=0), high, low)
        mine[...] = level
        gathered[me] = level
        start_bands(range(1, inner + 1))

        def begin(step, carry):
            gather_copy(mine, gathered, gather_send, gather_receive, step, size_x, size_y).start()
            return carry

        lax.fori_loop(1, devices, begin, 0)

        box_row = side * 8
        shifted[1, box_row : box_row + rows] = flat
        table = near_lookup()
        chunk = 256 if width % 256 == 0 else 128

        def near_term(a, b, columns, begin, end):
            slot, flipped = table[(a, b)]
            piece = shifted[1 + b, begin * box_row : end * box_row]
            if flipped:
                return product(piece, near[slot, columns, :], 0)
            return product(piece, near[slot, :, columns])

        def own_columns(index, carry):
            columns = pl.ds(pl.multiple_of(index * chunk, chunk), chunk)
            total[:, columns] = near_term(0, 0, columns, 1, side + 1)
            total[: rows - box_row, columns] += near_term(1, 0, columns, 2, side + 1)
            total[box_row:, columns] += near_term(-1, 0, columns, 1, side)
            return carry

        lax.fori_loop(0, width // chunk, own_columns, 0)
        finish_bands((0,))
        for b in (0, 2):
            shifted[b] = (
                padded[:, b : b + side]
                .astype(jnp.float32)
                .reshape((side + 2) * side * 8, width)
                .astype(jnp.bfloat16)
            )
        for x in (0, side + 1):
            shifted[1, x * box_row : (x + 1) * box_row] = (
                padded[x, 1 : 1 + side]
                .astype(jnp.float32)
                .reshape(box_row, width)
                .astype(jnp.bfloat16)
            )

        def near_columns(index, carry):
            columns = pl.ds(pl.multiple_of(index * chunk, chunk), chunk)
            value = total[:, columns]
            for a in (-1, 0, 1):
                for b in (-1, 1):
                    value = value + near_term(a, b, columns, 1 + a, 1 + a + side)
            total[:, columns] = value
            total[rows - box_row :, columns] += near_term(1, 0, columns, side + 1, side + 2)
            total[:box_row, columns] += near_term(-1, 0, columns, 0, 1)
            return carry

        lax.fori_loop(0, width // chunk, near_columns, 0)
        finish_bands(range(1, inner + 1))

        finish_gather(mine, gathered, gather_send, gather_receive)

        def couple(depth, window):
            value = None
            for k, (a, b) in enumerate(AROUND):
                span_rows = slice(4 * rank * k, 4 * rank * (k + 1))
                term = times(window(a, b), far_high[depth, span_rows], far_low[depth, span_rows])
                value = term if value is None else value + term
            return value

        across, along = size_x, size_y
        boxes = gathered[...].reshape(devices * 8, rank)
        for step in range(coarse):
            parents = group(boxes, across, along)
            across, along = across // 2, along // 2
            for i, parent in enumerate(parents):
                tops[step][1 + i // along, 1 + i % along] = parent
            if step < coarse - 1:
                high, low = halves(lifts[inner + step])
                boxes = times(jnp.concatenate(parents, axis=0), high, low)
        down = None
        for step in range(coarse - 1, -1, -1):
            near_x, near_y = me_x >> step + 1, me_y >> step + 1
            value = couple(
                inner + step, lambda a, b: tops[step][near_x + (1 + a), near_y + (1 + b)]
            )
            if down is not None:
                high, low = halves(lifts[inner + step])
                value = value + times(down, high, low, 0)
            child = 2 * (me_x >> step & 1) + (me_y >> step & 1)
            down = jnp.zeros((8, rank), jnp.float32)
            for i in range(4):
                down = jnp.where(child == i, value[:, i * rank : (i + 1) * rank], down)

        span = 1
        for depth in range(inner - 1, -1, -1):
            band = pyramid[depth]
            value = couple(
                depth,
                lambda a, b: band[1 + a : 1 + a + span, 1 + b : 1 + b + span].reshape(
                    span * span * 8, 4 * rank
                ),
            )
            high, low = halves(lifts[depth])
            value = value + times(down, high, low, 0)
            down = ungroup(value, span, span)
            span *= 2
        spread_down = product(stacked(down), basis[...])
        total[...] = total[...] + spread_down[:rows] + spread_down[rows:]

    boxes_of = side * 8

    def image_of(x, field):
        return field[x] + total[pl.ds(pl.multiple_of(x * boxes_of, 8), boxes_of)].reshape(
            side, 8, width
        )

    def wide_weight(x):
        return jnp.concatenate([weight[x]] * (width // weight.shape[3]), axis=-1)

    def set_first(x, carry):
        value = rhs[x] * inverse
        first[x] = value
        source[x] = (wide_weight(x) * value).astype(jnp.bfloat16)
        return carry

    inverse = 1.0 / beta
    lax.fori_loop(0, side, set_first, 0)
    near_copy.wait()
    operate()

    def first_sums(x):
        value, image = first[x], image_of(x, first)
        second[x] = image
        return rows_sum(value * image), rows_sum(image * image)

    start_sums(1, sweep(2, first_sums))
    h11, square = finish_sums(1, 2)
    h21 = jnp.sqrt(square - h11 * h11 + EPSILON)
    inverse_second = 1.0 / h21

    def set_second(x, carry):
        value = (second[x] - h11 * first[x]) * inverse_second
        second[x] = value
        source[x] = (wide_weight(x) * value).astype(jnp.bfloat16)
        return carry

    lax.fori_loop(0, side, set_second, 0)
    operate()

    def second_sums(x):
        image = image_of(x, second)
        third[x] = image
        return rows_sum(first[x] * image), rows_sum(second[x] * image), rows_sum(image * image)

    start_sums(2, sweep(3, second_sums))
    h12, h22, square = finish_sums(2, 3)
    h32 = jnp.sqrt(square - h12 * h12 - h22 * h22 + EPSILON)
    inverse_third = 1.0 / h32

    def set_third(x, carry):
        third[x] = (third[x] - h12 * first[x] - h22 * second[x]) * inverse_third
        return carry

    lax.fori_loop(0, side, set_third, 0)
    hess[...] = tile_of([beta, h11, h21, h12, h22, h32])


def krylov(rhs, weight, near, basis, lifts, coupling, count, size_x, size_y):
    side, _, _, width = rhs.shape
    rank = basis.shape[0]
    inner = side.bit_length() - 1
    levels = coupling.shape[0]
    coarse = levels - inner
    devices = size_x * size_y
    halos = inner + 1
    scratch = [
        pltpu.VMEM(near.shape, near.dtype),
        pltpu.VMEM((levels, 36 * rank, 4 * rank), jnp.bfloat16),
        pltpu.VMEM((levels, 36 * rank, 4 * rank), jnp.bfloat16),
        pltpu.VMEM(rhs.shape, jnp.float32),
        pltpu.VMEM(rhs.shape, jnp.float32),
        pltpu.VMEM(rhs.shape, jnp.bfloat16),
        pltpu.VMEM((side + 2, side + 2, 8, width), jnp.bfloat16),
    ]
    for depth in range(inner):
        span = (side >> depth + 1) + 2
        scratch.append(pltpu.VMEM((span, span, 8, 4 * rank), jnp.float32))
    for step in range(coarse):
        grid = ((size_x >> step + 1) + 2, (size_y >> step + 1) + 2)
        scratch.append(pltpu.VMEM(grid + (8, 4 * rank), jnp.float32))
    scratch += [
        pltpu.VMEM((8, rank), jnp.float32),
        pltpu.VMEM((devices, 8, rank), jnp.float32),
        pltpu.VMEM((3, (side + 2) * side * 8, width), jnp.bfloat16),
        pltpu.VMEM((side * side * 8, width), jnp.float32),
        pltpu.VMEM((3, 8, 128), jnp.float32),
        pltpu.VMEM((3, devices, 8, 128), jnp.float32),
        pltpu.SemaphoreType.DMA((halos, len(COMPASS))),
        pltpu.SemaphoreType.DMA((halos, len(COMPASS))),
        pltpu.SemaphoreType.DMA((devices,)),
        pltpu.SemaphoreType.DMA((devices,)),
        pltpu.SemaphoreType.DMA((3, devices)),
        pltpu.SemaphoreType.DMA((3, devices)),
        pltpu.SemaphoreType.DMA((1,)),
    ]
    return pl.pallas_call(
        functools.partial(krylov_kernel, size_x, size_y, inner, count),
        in_specs=[VMEM, VMEM, pl.BlockSpec(memory_space=pl.ANY), VMEM, VMEM, VMEM],
        out_specs=[VMEM, VMEM],
        out_shape=[
            jax.ShapeDtypeStruct(rhs.shape, jnp.float32),
            jax.ShapeDtypeStruct((8, 128), jnp.float32),
        ],
        scratch_shapes=scratch,
        compiler_params=pltpu.CompilerParams(collective_id=0, has_side_effects=True),
    )(rhs, weight, near, basis, lifts, coupling)


def body(rhs, contrast, occupied, near, basis, transfer, coupling):
    shape = rhs.shape
    side, _, fields, parts, voxels = shape
    width = parts * voxels
    rank = basis.shape[1]
    devices_x = lax.axis_size("gx")
    devices_y = lax.axis_size("gy")
    count = float(side * side * devices_x * devices_y * width)
    flat = rhs.reshape(side, side, fields, width)
    flat = jnp.pad(flat, ((0, 0), (0, 0), (0, 8 - fields), (0, 0)))
    weight = occupied.astype(jnp.float32)[:, :, None] * contrast
    weight = weight[:, :, None, :]
    lifts = transfer.reshape(transfer.shape[0], 4 * rank, rank)
    third, hess = krylov(
        flat, weight, near, basis.T, lifts, coupling, count, devices_x, devices_y
    )
    return (third[:, :, :fields].reshape(shape), hess[:fields, :6])


def solution(mesh):
    placed = (
        P("gx", "gy", None, None, None),
        P("gx", "gy", None),
        P("gx", "gy"),
        P(),
        P(),
        P(),
        P(),
    )
    return jax.shard_map(
        body,
        mesh=mesh,
        in_specs=placed,
        out_specs=(P("gx", "gy", None, None, None), P()),
        check_vma=False,
    )
```

```python
import functools

import jax
import jax.numpy as jnp
from jax import lax
from jax.experimental import pallas as pl
from jax.experimental.pallas import tpu as pltpu
from jax.sharding import PartitionSpec as P

EPSILON = 1e-06
NEAR_BASE = ((0, 0), (1, -1), (1, 0), (1, 1), (0, 1))
AROUND = [(a, b) for a in (-1, 0, 1) for b in (-1, 0, 1)]
COMPASS = [d for d in AROUND if d != (0, 0)]
MESH = pl.DeviceIdType.MESH
VMEM = pl.BlockSpec(memory_space=pltpu.VMEM)


def near_lookup():
    table = {}
    for slot, (a, b) in enumerate(NEAR_BASE):
        table[(a, b)] = (slot, False)
        if (a, b) != (0, 0):
            table[(-a, -b)] = (slot, True)
    return table


def far_lookup():
    base = [
        (a, b)
        for a in range(-3, 4)
        for b in range(-3, 4)
        if max(abs(a), abs(b)) >= 2 and (a > 0 or (a == 0 and b > 0))
    ]
    table = {}
    for slot, (a, b) in enumerate(base):
        table[(a, b)] = (slot, False)
        table[(-a, -b)] = (slot, True)
    return table


def halves(values):
    high = values.astype(jnp.bfloat16)
    return high, (values - high.astype(jnp.float32)).astype(jnp.bfloat16)


def far_level(depth, coupling, high, low):
    table = far_lookup()
    rank = coupling.shape[2]
    children = [(c, e) for c in (0, 1) for e in (0, 1)]
    empty = jnp.zeros((rank, rank), jnp.float32)
    row = 0
    for px, py in AROUND:
        for c, e in children:
            line = []
            for tc, te in children:
                found = table.get((2 * px + c - tc, 2 * py + e - te))
                if found is None:
                    line.append(empty)
                else:
                    block = coupling[depth, found[0]]
                    line.append(block.T if found[1] else block)
            high[depth, row : row + rank, :], low[depth, row : row + rank, :] = halves(
                jnp.concatenate(line, axis=1)
            )
            row += rank


def place(index, size_y):
    return {"gx": index // size_y, "gy": index % size_y}


def greet_all(size_x, size_y):
    total = size_x * size_y
    me = lax.axis_index("gx") * size_y + lax.axis_index("gy")
    barrier = pltpu.get_barrier_semaphore()

    def greet(step, carry):
        other = (me + step) % total
        pl.semaphore_signal(
            barrier, inc=1, device_id=place(other, size_y), device_id_type=MESH
        )
        return carry

    lax.fori_loop(1, total, greet, 0)


def await_greetings(size_x, size_y):
    pl.semaphore_wait(pltpu.get_barrier_semaphore(), size_x * size_y - 1)


def gather_copy(source, target, send, receive, step, size_x, size_y):
    total = size_x * size_y
    me = lax.axis_index("gx") * size_y + lax.axis_index("gy")
    other = (me + step) % total
    return pltpu.make_async_remote_copy(
        src_ref=source,
        dst_ref=target.at[me],
        send_sem=send.at[step],
        recv_sem=receive.at[step],
        device_id=place(other, size_y),
        device_id_type=MESH,
    )


def strip(move, length):
    if move > 0:
        return pl.ds(length, 1), pl.ds(0, 1)
    if move < 0:
        return pl.ds(1, 1), pl.ds(length + 1, 1)
    return pl.ds(1, length), pl.ds(1, length)


def stacked(values):
    high = values.astype(jnp.bfloat16).astype(jnp.float32)
    return jnp.concatenate([high, values - high], axis=0).astype(jnp.bfloat16)


def product(left, right, across=1):
    return lax.dot_general(
        left, right, (((1,), (1 - across,)), ((), ())), preferred_element_type=jnp.float32
    )


def times(values, high, low, across=1):
    both = stacked(values)
    total = product(both, high, across) + product(both, low, across)
    rows = values.shape[0]
    return total[:rows] + total[rows:]


def group(boxes, size_x, size_y):
    rows = []
    for x in range(0, size_x, 2):
        for y in range(0, size_y, 2):
            four = [(x + c) * size_y + y + e for c in (0, 1) for e in (0, 1)]
            rows.append(jnp.concatenate([boxes[8 * i : 8 * i + 8] for i in four], axis=1))
    return rows


def ungroup(parents, size_x, size_y):
    rank = parents.shape[1] // 4
    rows = []
    for x in range(2 * size_x):
        for y in range(2 * size_y):
            i = (x // 2) * size_y + y // 2
            k = 2 * (x % 2) + y % 2
            rows.append(parents[8 * i : 8 * i + 8, k * rank : (k + 1) * rank])
    return jnp.concatenate(rows, axis=0)


def clear_rim(out):
    long_x, long_y = out.shape[0], out.shape[1]
    line_x = jnp.zeros((1,) + out.shape[1:], out.dtype)
    line_y = jnp.zeros((long_x, 1) + out.shape[2:], out.dtype)
    out[0:1] = line_x
    out[long_x - 1 : long_x] = line_x
    out[:, 0:1] = line_y
    out[:, long_y - 1 : long_y] = line_y


def krylov_kernel(size_x, size_y, inner, count, *refs):
    rhs, weight, near_far_away, basis, lifts, coupling, third, hess = refs[:8]
    near, far_high, far_low, first, second, source = refs[8:14]
    padded = refs[14]
    pyramid = refs[15 : 15 + inner]
    rest = refs[15 + inner :]
    coarse = coupling.shape[0] - inner
    tops = rest[:coarse]
    mine, gathered, shifted, total, parts, slots = rest[coarse : coarse + 6]
    send, receive, gather_send, gather_receive, sum_send, sum_receive, load = rest[coarse + 6 :]
    side = source.shape[0]
    width = source.shape[3]
    rank = basis.shape[0]
    devices = size_x * size_y
    me_x, me_y = lax.axis_index("gx"), lax.axis_index("gy")
    me = me_x * size_y + me_y
    ways = range(len(COMPASS))
    bands = (padded,) + tuple(pyramid)
    rows = side * side * 8
    lane = lax.broadcasted_iota(jnp.int32, (8, 128), 1)

    def tile_of(columns):
        tile = jnp.zeros((8, 128), jnp.float32)
        for i, column in enumerate(columns):
            tile = jnp.where(lane == i, column, tile)
        return tile

    def start_sums(number, sums):
        tile = tile_of([jnp.sum(value, axis=1, keepdims=True) for value in sums])
        parts[number] = tile
        slots[number, me] = tile

        def begin(step, carry):
            gather_copy(
                parts.at[number],
                slots.at[number],
                sum_send.at[number],
                sum_receive.at[number],
                step,
                size_x,
                size_y,
            ).start()
            return carry

        lax.fori_loop(1, devices, begin, 0)

    def finish_gather(piece, target, sent, received):
        def finish(step, carry):
            other = (me + devices - step) % devices
            pltpu.make_async_remote_copy(
                src_ref=piece,
                dst_ref=target.at[other],
                send_sem=sent.at[step],
                recv_sem=received.at[step],
                device_id=place((me + step) % devices, size_y),
                device_id_type=MESH,
            ).wait()
            return carry

        lax.fori_loop(1, devices, finish, 0)

    def finish_sums(number, amount):
        finish_gather(
            parts.at[number], slots.at[number], sum_send.at[number], sum_receive.at[number]
        )
        tile = jnp.sum(slots[number], axis=0) / count
        return [tile[:, i : i + 1] for i in range(amount)]

    def rows_sum(value):
        return jnp.sum(value, axis=0)

    def sweep(amount, work):
        def one(x, sums):
            return tuple(old + new for old, new in zip(sums, work(x)))

        return lax.fori_loop(0, side, one, (jnp.zeros((8, width), jnp.float32),) * amount)

    near_copy = pltpu.make_async_copy(near_far_away, near, load.at[0])
    near_copy.start()
    for band in bands + tuple(tops):
        clear_rim(band)
    greet_all(size_x, size_y)

    def rhs_sums(x):
        pieces = [jnp.swapaxes(rhs[x, :, part], 0, 1) for part in range(rhs.shape[2])]
        value = jnp.concatenate(pieces, axis=-1)
        blank = jnp.zeros((side, 8 - rhs.shape[1], width), jnp.float32)
        value = jnp.concatenate([value, blank], axis=1)
        first[x] = value
        return (rows_sum(value * value),)

    sums = sweep(1, rhs_sums)
    await_greetings(size_x, size_y)
    start_sums(0, sums)

    def build(depth, carry):
        far_level(depth, coupling, far_high, far_low)
        return carry

    lax.fori_loop(0, coupling.shape[0], build, 0)
    (square,) = finish_sums(0, 1)
    beta = jnp.sqrt(square + EPSILON)

    def copy_of(number, way):
        move_x, move_y = COMPASS[way]
        band = bands[number]
        from_x, to_x = strip(move_x, band.shape[0] - 2)
        from_y, to_y = strip(move_y, band.shape[1] - 2)
        return pltpu.make_async_remote_copy(
            src_ref=band.at[from_x, from_y],
            dst_ref=band.at[to_x, to_y],
            send_sem=send.at[number, way],
            recv_sem=receive.at[number, way],
            device_id={"gx": me_x + move_x, "gy": me_y + move_y},
            device_id_type=MESH,
        )

    def inside(place_x, place_y):
        return (place_x >= 0) & (place_x < size_x) & (place_y >= 0) & (place_y < size_y)

    def start_bands(numbers):
        for way in ways:
            move_x, move_y = COMPASS[way]

            @pl.when(inside(me_x + move_x, me_y + move_y))
            def _(way=way):
                for number in numbers:
                    copy_of(number, way).start()

    def finish_bands(numbers):
        for way in ways:
            move_x, move_y = COMPASS[way]

            @pl.when(inside(me_x + move_x, me_y + move_y))
            def _(way=way):
                for number in numbers:
                    copy_of(number, way).wait_send()

            @pl.when(inside(me_x - move_x, me_y - move_y))
            def _(way=way):
                for number in numbers:
                    copy_of(number, way).wait_recv()

    def operate():
        padded[1 : 1 + side, 1 : 1 + side] = source[...]
        start_bands((0,))

        flat = source[...].astype(jnp.float32).reshape(side * side * 8, width).astype(jnp.bfloat16)
        level = product(flat, basis[...], 0)
        span = side
        for depth in range(inner):
            parents = group(level, span, span)
            span //= 2
            for i, parent in enumerate(parents):
                pyramid[depth][1 + i // span, 1 + i % span] = parent
            high, low = halves(lifts[depth])
            level = times(jnp.concatenate(parents, axis=0), high, low)
        mine[...] = level
        gathered[me] = level
        start_bands(range(1, inner + 1))

        def begin(step, carry):
            gather_copy(mine, gathered, gather_send, gather_receive, step, size_x, size_y).start()
            return carry

        lax.fori_loop(1, devices, begin, 0)

        box_row = side * 8
        shifted[1, box_row : box_row + rows] = flat
        table = near_lookup()
        chunk = 256 if width % 256 == 0 else 128

        def near_term(a, b, columns, begin, end):
            slot, flipped = table[(a, b)]
            piece = shifted[1 + b, begin * box_row : end * box_row]
            if flipped:
                return product(piece, near[slot, columns, :], 0)
            return product(piece, near[slot, :, columns])

        def own_columns(index, carry):
            columns = pl.ds(pl.multiple_of(index * chunk, chunk), chunk)
            total[:, columns] = near_term(0, 0, columns, 1, side + 1)
            total[: rows - box_row, columns] += near_term(1, 0, columns, 2, side + 1)
            total[box_row:, columns] += near_term(-1, 0, columns, 1, side)
            return carry

        lax.fori_loop(0, width // chunk, own_columns, 0)
        finish_bands((0,))
        for b in (0, 2):
            shifted[b] = (
                padded[:, b : b + side]
                .astype(jnp.float32)
                .reshape((side + 2) * side * 8, width)
                .astype(jnp.bfloat16)
            )
        for x in (0, side + 1):
            shifted[1, x * box_row : (x + 1) * box_row] = (
                padded[x, 1 : 1 + side]
                .astype(jnp.float32)
                .reshape(box_row, width)
                .astype(jnp.bfloat16)
            )

        def near_columns(index, carry):
            columns = pl.ds(pl.multiple_of(index * chunk, chunk), chunk)
            value = total[:, columns]
            for a in (-1, 0, 1):
                for b in (-1, 1):
                    value = value + near_term(a, b, columns, 1 + a, 1 + a + side)
            total[:, columns] = value
            total[rows - box_row :, columns] += near_term(1, 0, columns, side + 1, side + 2)
            total[:box_row, columns] += near_term(-1, 0, columns, 0, 1)
            return carry

        lax.fori_loop(0, width // chunk, near_columns, 0)
        finish_bands(range(1, inner + 1))

        finish_gather(mine, gathered, gather_send, gather_receive)

        def couple(depth, window):
            value = None
            for k, (a, b) in enumerate(AROUND):
                span_rows = slice(4 * rank * k, 4 * rank * (k + 1))
                term = times(window(a, b), far_high[depth, span_rows], far_low[depth, span_rows])
                value = term if value is None else value + term
            return value

        across, along = size_x, size_y
        boxes = gathered[...].reshape(devices * 8, rank)
        for step in range(coarse):
            parents = group(boxes, across, along)
            across, along = across // 2, along // 2
            for i, parent in enumerate(parents):
                tops[step][1 + i // along, 1 + i % along] = parent
            if step < coarse - 1:
                high, low = halves(lifts[inner + step])
                boxes = times(jnp.concatenate(parents, axis=0), high, low)
        down = None
        for step in range(coarse - 1, -1, -1):
            near_x, near_y = me_x >> step + 1, me_y >> step + 1
            value = couple(
                inner + step, lambda a, b: tops[step][near_x + (1 + a), near_y + (1 + b)]
            )
            if down is not None:
                high, low = halves(lifts[inner + step])
                value = value + times(down, high, low, 0)
            child = 2 * (me_x >> step & 1) + (me_y >> step & 1)
            down = jnp.zeros((8, rank), jnp.float32)
            for i in range(4):
                down = jnp.where(child == i, value[:, i * rank : (i + 1) * rank], down)

        span = 1
        for depth in range(inner - 1, -1, -1):
            band = pyramid[depth]
            value = couple(
                depth,
                lambda a, b: band[1 + a : 1 + a + span, 1 + b : 1 + b + span].reshape(
                    span * span * 8, 4 * rank
                ),
            )
            high, low = halves(lifts[depth])
            value = value + times(down, high, low, 0)
            down = ungroup(value, span, span)
            span *= 2
        spread_down = product(stacked(down), basis[...])
        total[...] = total[...] + spread_down[:rows] + spread_down[rows:]

    boxes_of = side * 8

    def image_of(x, field):
        return field[x] + total[pl.ds(pl.multiple_of(x * boxes_of, 8), boxes_of)].reshape(
            side, 8, width
        )

    def wide_weight(x):
        return jnp.concatenate([weight[x]] * (width // weight.shape[3]), axis=-1)

    def set_first(x, carry):
        value = first[x] * inverse
        first[x] = value
        source[x] = (wide_weight(x) * value).astype(jnp.bfloat16)
        return carry

    inverse = 1.0 / beta
    lax.fori_loop(0, side, set_first, 0)
    near_copy.wait()
    operate()

    def first_sums(x):
        value, image = first[x], image_of(x, first)
        second[x] = image
        return rows_sum(value * image), rows_sum(image * image)

    start_sums(1, sweep(2, first_sums))
    h11, square = finish_sums(1, 2)
    h21 = jnp.sqrt(square - h11 * h11 + EPSILON)
    inverse_second = 1.0 / h21

    def set_second(x, carry):
        value = (second[x] - h11 * first[x]) * inverse_second
        second[x] = value
        source[x] = (wide_weight(x) * value).astype(jnp.bfloat16)
        return carry

    lax.fori_loop(0, side, set_second, 0)
    operate()

    def second_sums(x):
        image = image_of(x, second)
        third[x] = image
        return rows_sum(first[x] * image), rows_sum(second[x] * image), rows_sum(image * image)

    start_sums(2, sweep(3, second_sums))
    h12, h22, square = finish_sums(2, 3)
    h32 = jnp.sqrt(square - h12 * h12 - h22 * h22 + EPSILON)
    inverse_third = 1.0 / h32

    def set_third(x, carry):
        third[x] = (third[x] - h12 * first[x] - h22 * second[x]) * inverse_third
        return carry

    lax.fori_loop(0, side, set_third, 0)
    hess[...] = tile_of([beta, h11, h21, h12, h22, h32])


def krylov(rhs, weight, near, basis, lifts, coupling, count, size_x, size_y):
    side = rhs.shape[0]
    rank, width = basis.shape
    boxes = (side, side, 8, width)
    inner = side.bit_length() - 1
    levels = coupling.shape[0]
    coarse = levels - inner
    devices = size_x * size_y
    halos = inner + 1
    scratch = [
        pltpu.VMEM(near.shape, near.dtype),
        pltpu.VMEM((levels, 36 * rank, 4 * rank), jnp.bfloat16),
        pltpu.VMEM((levels, 36 * rank, 4 * rank), jnp.bfloat16),
        pltpu.VMEM(boxes, jnp.float32),
        pltpu.VMEM(boxes, jnp.float32),
        pltpu.VMEM(boxes, jnp.bfloat16),
        pltpu.VMEM((side + 2, side + 2, 8, width), jnp.bfloat16),
    ]
    for depth in range(inner):
        span = (side >> depth + 1) + 2
        scratch.append(pltpu.VMEM((span, span, 8, 4 * rank), jnp.float32))
    for step in range(coarse):
        grid = ((size_x >> step + 1) + 2, (size_y >> step + 1) + 2)
        scratch.append(pltpu.VMEM(grid + (8, 4 * rank), jnp.float32))
    scratch += [
        pltpu.VMEM((8, rank), jnp.float32),
        pltpu.VMEM((devices, 8, rank), jnp.float32),
        pltpu.VMEM((3, (side + 2) * side * 8, width), jnp.bfloat16),
        pltpu.VMEM((side * side * 8, width), jnp.float32),
        pltpu.VMEM((3, 8, 128), jnp.float32),
        pltpu.VMEM((3, devices, 8, 128), jnp.float32),
        pltpu.SemaphoreType.DMA((halos, len(COMPASS))),
        pltpu.SemaphoreType.DMA((halos, len(COMPASS))),
        pltpu.SemaphoreType.DMA((devices,)),
        pltpu.SemaphoreType.DMA((devices,)),
        pltpu.SemaphoreType.DMA((3, devices)),
        pltpu.SemaphoreType.DMA((3, devices)),
        pltpu.SemaphoreType.DMA((1,)),
    ]
    return pl.pallas_call(
        functools.partial(krylov_kernel, size_x, size_y, inner, count),
        in_specs=[VMEM, VMEM, pl.BlockSpec(memory_space=pl.ANY), VMEM, VMEM, VMEM],
        out_specs=[VMEM, VMEM],
        out_shape=[
            jax.ShapeDtypeStruct(boxes, jnp.float32),
            jax.ShapeDtypeStruct((8, 128), jnp.float32),
        ],
        scratch_shapes=scratch,
        compiler_params=pltpu.CompilerParams(collective_id=0, has_side_effects=True),
    )(rhs, weight, near, basis, lifts, coupling)


def body(rhs, contrast, occupied, near, basis, transfer, coupling):
    shape = rhs.shape
    side, _, fields, parts, voxels = shape
    width = parts * voxels
    rank = basis.shape[1]
    devices_x = lax.axis_size("gx")
    devices_y = lax.axis_size("gy")
    count = float(side * side * devices_x * devices_y * width)
    flat = rhs.transpose(0, 2, 3, 1, 4)
    weight = occupied.astype(jnp.float32)[:, :, None] * contrast
    weight = weight[:, :, None, :]
    lifts = transfer.reshape(transfer.shape[0], 4 * rank, rank)
    third, hess = krylov(
        flat, weight, near, basis.T, lifts, coupling, count, devices_x, devices_y
    )
    return (third[:, :, :fields].reshape(shape), hess[:fields, :6])


def solution(mesh):
    placed = (
        P("gx", "gy", None, None, None),
        P("gx", "gy", None),
        P("gx", "gy"),
        P(),
        P(),
        P(),
        P(),
    )
    return jax.shard_map(
        body,
        mesh=mesh,
        in_specs=placed,
        out_specs=(P("gx", "gy", None, None, None), P()),
        check_vma=False,
    )
```
